512 devices in a mesh: dp: 16 (over x, z_lo), expert: 32 (over y, z_hi, core).
Axes of the slice: x: 4, y: 4, z: 16 (z_hi: 4, z_lo: 4; z = z_hi * 4 + z_lo), core: 2. Of those that a mesh axis runs over, the one named last changes fastest.
Arguments:
- tokens: bfloat16 [4096, 2560], P(('dp', 'expert')), may hold values from -24 to 24
- routes: int32 [4096, 6], P(('dp', 'expert')), may hold values from 0 to 7, all different within a row; in each aligned block of 8 rows (0 to 7, 8 to 15, ...) at most 7 rows name the same one
- router: float32 [2560, 8], replicated, may hold values from -0.125 to 0.125
- w_gate: bfloat16 [2560, 8192], P(None, 'expert'), may hold values from -0.125 to 0.125
- w_up: bfloat16 [2560, 8192], P(None, 'expert'), may hold values from -0.125 to 0.125
- w_down: bfloat16 [2560, 8192], P(None, 'expert'), may hold values from -0.1875 to 0.1875
- cotangent: bfloat16 [4096, 2560], P(('dp', 'expert')), may hold values from -6 to 6
Outputs:
- mixed: bfloat16 [4096, 2560], P(('dp', 'expert'))
- grad_tokens: bfloat16 [4096, 2560], P(('dp', 'expert'))
- grad_router: float32 [2560, 8], replicated
- grad_gate: float32 [2560, 8192], P('dp', 'expert')
- grad_up: float32 [2560, 8192], P('dp', 'expert')
- grad_down: float32 [2560, 8192], P('dp', 'expert')
The draws below stay inside these ranges and needn't reach their ends.
Inputs may be any that keep to these rules, and one draw needn't show every extreme that they name: `routes`: each row names 6 different experts. Among the rows of one device no expert is named more than 7 times, and in every draw some expert is named exactly 7 times by the rows of some device.
All inputs are finite; a program needn't handle non-finite values.
Results may differ from the reference program's by a relative error of at most 0.02.
Values may be sent and summed in bfloat16 or wider, within the bound.
A program may use at most 64 MiB of HBM per device.

```python
import math
import jax
import jax.numpy as jnp
import numpy as np
from jax import lax

D = 2560
FFW = 1024
TOP = 6
EXPERTS = 8
TOK_DEV = 8
HSPLIT = 4
FF_DEV = 256
TOKENS = 4096
CAP = 7
N_DP = 16
N_EXPERT = 32


def strengthened(result, stream_key, source, target, blocks, factor):
    owner, partner = [(jnp.arange(result.shape[dim]) // (result.shape[dim] // blocks)).reshape([-1 if axis == dim else 1 for axis in range(result.ndim)]) for dim in (source, target)]
    chosen = jax.random.permutation(stream_key, blocks)[partner]
    strong = (owner == chosen) | (owner == (partner + blocks // 2) % blocks)
    return jnp.where(strong, factor * result, result)


def steps_of(rng, shape, split, least, largest):
    gain, own = 1.0, jax.random.fold_in(rng, 6)
    for dim, blocks in split:
        draws = jnp.exp(jax.random.uniform(jax.random.fold_in(own, dim), (blocks,), jnp.float32, least / len(split), largest / len(split)))
        gain = gain * jnp.repeat(draws, shape[dim] // blocks).reshape([-1 if axis == dim else 1 for axis in range(len(shape))])
    return gain


def deal_out(own_key, own, number, rows, count, top, limit, slope):
    order = jax.random.permutation(own_key, count)
    crowded, usual = portions_of(count, rows * top, limit, slope, True), portions_of(count, rows * top, limit, slope, False)
    places = jnp.arange(count)

    def named(lengths, offset_by):
        used = int((lengths > 0).sum())
        fixed = max(1, used // 4)
        moved = fixed + (places - fixed + offset_by * (used - fixed)) % max(1, count - fixed)
        return jnp.zeros((count,), jnp.int32).at[order[jnp.where(places < fixed, places, moved)]].set(jnp.asarray(lengths, jnp.int32))

    lengths = jnp.where(number % 4 == 0, named(crowded, number // 4), named(usual, number - number // 4 - 1))
    mixed = jax.random.permutation(jax.random.fold_in(own, 3), count)
    source_of, receiver = mixed[0:count // 2 * 2:2], mixed[1:count // 2 * 2:2]
    room = jnp.minimum(lengths[source_of] - 1, limit - lengths[receiver]) // 2
    room = jnp.where((source_of == order[0]) | (receiver == order[0]) | (lengths[receiver] == 0), 0, jnp.maximum(room, 0))
    moved = jax.random.randint(jax.random.fold_in(own, 4), (count // 2,), 0, 1 << 20) % (room + 1)
    lengths = lengths.at[source_of].add(-moved).at[receiver].add(moved)
    members = jnp.searchsorted(jnp.cumsum(lengths), jnp.arange(rows * top), side="right").astype(jnp.int32)
    table = members.reshape(top, rows).T
    table = table[jax.random.permutation(jax.random.fold_in(own, 1), rows)]
    offset_by = jax.random.randint(jax.random.fold_in(own, 2), (rows, 1), 0, top)
    return jnp.take_along_axis(table, (jnp.arange(top)[None, :] + offset_by) % top, axis=1)


def portions_of(number_of, total, most, skew, full):
    weights = [(1 << 20) // math.isqrt(rank ** skew) + 1 for rank in range(1, number_of + 1)]
    largest = most if full else min(most, max(-(-total // number_of), total * weights[0] // sum(weights)))
    least = 1 if total - largest >= number_of - 1 else 0
    counts, surplus = [largest] + [least] * (number_of - 1), total - largest - least * (number_of - 1)
    while surplus > 0:
        candidates = [i for i in range(1, number_of) if counts[i] < largest] or [i for i in range(1, number_of) if counts[i] < most]
        whole, remaining = sum([weights[i] for i in candidates]), surplus
        for i in candidates:
            more = min(most - counts[i], max(1, remaining * weights[i] // whole), surplus)
            counts[i] = counts[i] + more
            surplus = surplus - more
    return np.array(counts)


def bell_draw(own_key, dims, width, reach, pieces=(), held_as=jnp.bfloat16):
    level = steps_of(own_key, dims, pieces, -0.22, 0.18) if pieces else 1.0
    drawn = jax.random.normal(own_key, dims, jnp.float32) * width * level
    return jnp.minimum(jnp.maximum(drawn, -reach), reach).astype(held_as)


def noise_with(rng, dims, scale, reach, pieces, heavy, kind=jnp.bfloat16):
    drawn = scale * jax.random.normal(rng, dims, jnp.float32)
    if pieces:
        drawn = drawn * steps_of(rng, dims, pieces, -0.22, 0.18)
    return jnp.clip(strengthened(drawn, jax.random.fold_in(rng, 3), *heavy), -reach, reach).astype(kind)


def setup_inputs(seed: int = 0) -> dict:
    seeds = jax.random.split(jax.random.key(seed), 8)
    tokens = noise_with(seeds[0], (TOKENS, D), 1.0, 24.0, ((0, 512),), (0, 1, 512, 6.0))
    routes_keys = jax.random.split(jax.random.fold_in(seeds[1], 1), TOKENS // TOK_DEV)
    routes_turns = jax.random.permutation(jax.random.fold_in(seeds[1], 3), TOKENS // TOK_DEV)
    routes = jax.vmap(lambda own, number: deal_out(jax.random.fold_in(seeds[1], 2), own, number, TOK_DEV, EXPERTS, TOP, CAP, 2))(routes_keys, routes_turns).reshape((TOKENS, TOP))
    router = bell_draw(seeds[2], (D, EXPERTS), D ** -0.5, 0.125, (), jnp.float32)
    w_gate = bell_draw(seeds[3], (D, EXPERTS * FFW), D ** -0.5, 0.125, ((1, 32),))
    w_up = bell_draw(seeds[4], (D, EXPERTS * FFW), D ** -0.5, 0.125, ((1, 32),))
    w_down = bell_draw(seeds[5], (D, EXPERTS * FFW), FFW ** -0.5, 0.1875, ((1, 32),))
    cotangent = bell_draw(seeds[6], (TOKENS, D), 1.0, 6.0, ((0, 512),))
    return {"tokens": tokens, "routes": routes, "router": router, "w_gate": w_gate, "w_up": w_up, "w_down": w_down, "cotangent": cotangent}


def expert_hidden(inputs, gate_matrix, up_matrix):
    gate_pre = jnp.dot(inputs, gate_matrix, preferred_element_type=jnp.float32)
    up_pre = jnp.dot(inputs, up_matrix, preferred_element_type=jnp.float32)
    hidden = (jax.nn.silu(gate_pre) * up_pre).astype(jnp.bfloat16)
    return gate_pre, up_pre, hidden


def block_down(hidden, down_matrix):
    total = jnp.zeros((hidden.shape[0], D), jnp.float32)
    for block in range(HSPLIT):
        lo = block * FF_DEV
        piece = jnp.dot(hidden[:, lo:lo + FF_DEV], down_matrix[:, lo:lo + FF_DEV].T,
                        preferred_element_type=jnp.float32).astype(jnp.bfloat16)
        total = total + lax.optimization_barrier(piece).astype(jnp.float32)
    return total.astype(jnp.bfloat16)


def expert_backward(slot_grad, gate_pre, up_pre, gate_matrix, up_matrix, down_matrix):
    hidden_grad = jnp.dot(slot_grad, down_matrix, preferred_element_type=jnp.float32)
    sigma = jax.nn.sigmoid(gate_pre)
    gate_grad = (hidden_grad * up_pre * sigma * (1.0 + gate_pre * (1.0 - sigma))).astype(jnp.bfloat16)
    up_grad = (hidden_grad * gate_pre * sigma).astype(jnp.bfloat16)
    total = jnp.zeros((slot_grad.shape[0], D), jnp.float32)
    for block in range(HSPLIT):
        lo = block * FF_DEV
        piece = jnp.dot(gate_grad[:, lo:lo + FF_DEV], gate_matrix[:, lo:lo + FF_DEV].T, preferred_element_type=jnp.float32)
        piece = piece + jnp.dot(up_grad[:, lo:lo + FF_DEV], up_matrix[:, lo:lo + FF_DEV].T, preferred_element_type=jnp.float32)
        total = total + lax.optimization_barrier(piece.astype(jnp.bfloat16)).astype(jnp.float32)
    return gate_grad, up_grad, total.astype(jnp.bfloat16)


def stacked(weight):
    return weight.reshape(D, EXPERTS, FFW).transpose(1, 0, 2)


def unstacked(grad):
    return grad.transpose(1, 0, 2).reshape(D, EXPERTS * FFW)


def group_sum(left, right):
    group_rows = N_EXPERT * CAP
    left_wide = left.astype(jnp.float32).reshape(N_DP, group_rows, left.shape[1])
    right_wide = right.astype(jnp.float32).reshape(N_DP, group_rows, right.shape[1])
    parts = jnp.einsum("grd,grf->gdf", left_wide, right_wide, precision=lax.Precision.HIGHEST)
    return jnp.sum(parts.astype(jnp.bfloat16).astype(jnp.float32), axis=0)


def reference(tokens, routes, router, w_gate, w_up, w_down, cotangent):
    blocks = TOKENS // TOK_DEV
    highest = lax.Precision.HIGHEST
    tokens_wide = tokens.astype(jnp.float32)
    logits = jnp.dot(tokens_wide, router, precision=highest)
    expert_ids = jnp.arange(EXPERTS, dtype=jnp.int32)
    choose = routes[:, :, None] == expert_ids[None, None, :]
    choose_f = choose.astype(jnp.float32)
    picked = jnp.sum(choose_f * logits[:, None, :], axis=2)
    affinity = jax.nn.sigmoid(picked)
    denominator = jnp.sum(affinity, axis=1, keepdims=True)
    gate_values = affinity / denominator

    choose_i = choose.astype(jnp.int32).reshape(blocks, TOK_DEV, TOP, EXPERTS)
    per_token = jnp.sum(choose_i, axis=2)
    before = jnp.cumsum(per_token, axis=1) - per_token
    position = jnp.sum(choose_i * before[:, :, None, :], axis=3).reshape(TOKENS, TOP)
    block_index = (jnp.arange(TOKENS, dtype=jnp.int32) // TOK_DEV)[:, None]
    flat_slot = routes * (blocks * CAP) + block_index * CAP + position
    slot_total = EXPERTS * blocks * CAP
    sources = jnp.full((slot_total + 1,), TOKENS * TOP, dtype=jnp.int32)
    sources = sources.at[flat_slot.reshape(-1)].set(jnp.arange(TOKENS * TOP, dtype=jnp.int32))
    sources = sources[:slot_total].reshape(EXPERTS, blocks * CAP)

    tokens_pad = jnp.concatenate([tokens, jnp.zeros((1, D), jnp.bfloat16)], axis=0)
    cotangent_pad = jnp.concatenate([cotangent, jnp.zeros((1, D), jnp.bfloat16)], axis=0)
    gates_pad = jnp.concatenate([gate_values.reshape(-1), jnp.zeros((1,), jnp.float32)], axis=0)

    def expert_step(carry, inputs):
        mixed_acc, input_acc, pull_acc = carry
        gate_matrix, up_matrix, down_matrix, slot_source = inputs
        token_of = slot_source // TOP
        expert_rows = tokens_pad[token_of]
        grad_rows = cotangent_pad[token_of]
        slot_gate = gates_pad[slot_source]
        gate_pre, up_pre, hidden = expert_hidden(expert_rows, gate_matrix, up_matrix)
        output = block_down(hidden, down_matrix)
        output_wide = lax.optimization_barrier(output).astype(jnp.float32)
        mixed_acc = mixed_acc.at[token_of].add(slot_gate[:, None] * output_wide)
        pull_acc = pull_acc.at[slot_source].set(jnp.sum(grad_rows.astype(jnp.float32) * output_wide, axis=1))
        slot_grad = (slot_gate[:, None] * grad_rows.astype(jnp.float32)).astype(jnp.bfloat16)
        gate_grad, up_grad, input_grad = expert_backward(slot_grad, gate_pre, up_pre, gate_matrix, up_matrix, down_matrix)
        input_acc = input_acc.at[token_of].add(lax.optimization_barrier(input_grad).astype(jnp.float32))
        part_gate = group_sum(expert_rows, gate_grad)
        part_up = group_sum(expert_rows, up_grad)
        part_down = group_sum(slot_grad, hidden)
        return (mixed_acc, input_acc, pull_acc), (part_gate, part_up, part_down)

    start_carry = (jnp.zeros((TOKENS + 1, D), jnp.float32), jnp.zeros((TOKENS + 1, D), jnp.float32),
                   jnp.zeros((TOKENS * TOP + 1,), jnp.float32))
    final_carry, grads = lax.scan(expert_step, start_carry,
                                  (stacked(w_gate), stacked(w_up), stacked(w_down), sources))
    mixed_acc, input_acc, pull_acc = final_carry
    grad_gate, grad_up, grad_down = grads

    mixed = mixed_acc[:TOKENS].astype(jnp.bfloat16)
    gate_pull = pull_acc[:TOKENS * TOP].reshape(TOKENS, TOP)
    mean_pull = jnp.sum(gate_values * gate_pull, axis=1, keepdims=True)
    logit_grad = (gate_pull - mean_pull) / denominator * affinity * (1.0 - affinity)
    per_logit = jnp.sum(choose_f * logit_grad[:, :, None], axis=1)
    grad_router = jnp.dot(tokens_wide.T, per_logit, precision=highest)
    router_back = jnp.dot(per_logit, router.T, precision=highest)
    grad_tokens = (input_acc[:TOKENS] + router_back).astype(jnp.bfloat16)
    return (mixed, grad_tokens, grad_router, unstacked(grad_gate), unstacked(grad_up), unstacked(grad_down))
```

```python
import functools

import jax
import jax.numpy as jnp
from jax import lax
from jax.experimental import pallas as pl
from jax.experimental.pallas import tpu as pltpu
from jax.sharding import PartitionSpec as P

NY = 4
NZ = 4
MESH = pl.DeviceIdType.MESH
VMEM = pl.BlockSpec(memory_space=pltpu.VMEM)
F32 = jnp.float32
BF16 = jnp.bfloat16


def greet(axis, peers):
    barrier = pltpu.get_barrier_semaphore()
    for peer in peers:
        pl.semaphore_signal(barrier, inc=1, device_id={axis: peer}, device_id_type=MESH)
    pl.semaphore_wait(barrier, len(peers))


def group_place():
    j = lax.axis_index("expert")
    core = lax.rem(j, 2)
    zh = lax.rem(lax.div(j, 2), NZ)
    y = lax.div(j, 2 * NZ)
    return j, y, zh, core


def member(y, zh, core):
    return (lax.rem(y, NY) * NZ + lax.rem(zh, NZ)) * 2 + core


def gather_kernel(x_ref, c_ref, m_ref, xo, co, mo, send_sem, recv_sem, local_sem):
    j, y, zh, core = group_place()
    z_up, z_down = member(y, zh + 1, core), member(y, zh + 3, core)
    y_up, y_down = member(y + 1, zh, core), member(y + 3, zh, core)
    twin = member(y, zh, 1 - core)
    greet("expert", (z_up, z_down, y_up, y_down, twin))
    ins, outs = (x_ref, c_ref, m_ref), (xo, co, mo)
    used = [0, 0, 0]
    sent = []

    def send(a, block, target, own=False):
        copy = pltpu.make_async_remote_copy(
            src_ref=ins[a] if own else outs[a].at[block],
            dst_ref=outs[a].at[block],
            send_sem=send_sem.at[a, used[a]],
            recv_sem=recv_sem.at[a, block],
            device_id={"expert": target},
            device_id_type=MESH,
        )
        used[a] += 1
        copy.start()
        sent.append(copy)

    def arrive(a, block):
        pltpu.make_async_remote_copy(
            src_ref=outs[a].at[block],
            dst_ref=outs[a].at[block],
            send_sem=send_sem.at[a, 0],
            recv_sem=recv_sem.at[a, block],
            device_id={"expert": twin},
            device_id_type=MESH,
        ).wait_recv()

    def at(dy, dz):
        return member(y + dy, zh + dz, core)

    for a in (0, 2, 1):
        send(a, j, z_up, True)
        send(a, j, z_down, True)
    for a in (0, 2, 1):
        send(a, j, y_up, True)
        send(a, j, y_down, True)
        send(a, j, twin, True)
    held = [pltpu.make_async_copy(ins[a], outs[a].at[j], local_sem.at[a]) for a in range(3)]
    for copy in held:
        copy.start()

    def spread(a, dz):
        block = at(0, dz)
        send(a, block, y_up)
        send(a, block, y_down)
        send(a, block, twin)

    def side(dz):
        for a in (0, 2):
            arrive(a, at(3, dz))
            send(a, at(3, dz), y_up)
            send(a, at(3, dz), twin)
        arrive(1, at(1, dz))
        send(1, at(1, dz), y_down)
        send(1, at(1, dz), twin)
        for a in (0, 2):
            arrive(a, at(1, dz))
            send(a, at(1, dz), twin)
        arrive(1, at(3, dz))
        send(1, at(3, dz), twin)

    def far(dz):
        for a in (0, 2, 1):
            arrive(a, at(2, dz))
            send(a, at(2, dz), twin)

    for a in (0, 2):
        arrive(a, at(0, 3))
        send(a, at(0, 3), z_up)
        spread(a, 3)
    for a in (0, 2):
        arrive(a, at(0, 1))
        spread(a, 1)
    arrive(1, at(0, 1))
    send(1, at(0, 1), z_down)
    spread(1, 1)
    arrive(1, at(0, 3))
    spread(1, 3)
    side(0)
    for a in (0, 2, 1):
        arrive(a, at(0, 2))
        spread(a, 2)
    far(0)
    side(3)
    side(1)
    far(3)
    far(1)
    side(2)
    far(2)
    for i in range(NY * NZ):
        for a in range(3):
            arrive(a, 2 * i + 1 - core)
    for copy in held:
        copy.wait()
    for copy in sent:
        copy.wait_send()


def gather(x, c, m):
    shapes = [jax.ShapeDtypeStruct((2 * NY * NZ, *a.shape), a.dtype) for a in (x, c, m)]
    return pl.pallas_call(
        gather_kernel,
        out_shape=shapes,
        in_specs=[VMEM] * 3,
        out_specs=[VMEM] * 3,
        scratch_shapes=[
            pltpu.SemaphoreType.DMA((3, 31)),
            pltpu.SemaphoreType.DMA((3, 32)),
            pltpu.SemaphoreType.DMA((3,)),
        ],
        compiler_params=pltpu.CompilerParams(collective_id=0, has_side_effects=True),
        name="group_gather",
    )(x, c, m)


def remote(src, dst, send_sem, recv_sem, axis, target):
    return pltpu.make_async_remote_copy(
        src_ref=src, dst_ref=dst, send_sem=send_sem, recv_sem=recv_sem,
        device_id={axis: target}, device_id_type=MESH,
    )


def return_kernel(pm, pn, gp, mo, no, go, cbuf, q, s1, fy, r, s1z, fz, r2,
                  cs, cr, ys, yr, zs, zr, gs, gr, gl):
    j, y, zh, core = group_place()
    z_up, z_down = member(y, zh + 1, core), member(y, zh + 3, core)
    y_up, y_down = member(y + 1, zh, core), member(y + 3, zh, core)
    twin = member(y, zh, 1 - core)
    total = 2 * NY * NZ
    barrier = pltpu.get_barrier_semaphore()

    @pl.loop(1, total)
    def _(i):
        pl.semaphore_signal(barrier, inc=1, device_id={"expert": lax.rem(j + i, total)},
                            device_id_type=MESH)

    pl.semaphore_wait(barrier, total - 1)
    parts = (pm, pn)
    sent = []

    def go_on(copy):
        copy.start()
        sent.append(copy)
        return copy

    core_copy = {}
    for dy in (2, 1, 3, 0):
        yy = lax.rem(y + dy, NY)
        for a in range(2):
            core_copy[a, dy] = go_on(remote(parts[a].at[yy, :, 1 - core], cbuf.at[a, yy],
                                            cs.at[a, dy], cr.at[a, yy], "expert", twin))

    def pull_copy(i):
        peer = lax.rem(j + i, total)
        return remote(gp, go.at[j], gs.at[i], gr.at[j], "expert", peer)

    @pl.loop(1, total)
    def _(i):
        pull_copy(i).start()

    keep = pltpu.make_async_copy(gp, go.at[j], gl)
    keep.start()

    def add_core(a, dy):
        yy = lax.rem(y + dy, NY)
        remote(cbuf.at[a, yy], cbuf.at[a, yy], cs.at[a, dy], cr.at[a, yy], "expert", twin).wait_recv()

        @pl.loop(0, NZ)
        def _(k):
            q[a, yy, k] = (parts[a][yy, k, core].astype(F32) + cbuf[a, yy, k].astype(F32)).astype(BF16)

    y2, y1, y3 = lax.rem(y + 2, NY), lax.rem(y + 1, NY), lax.rem(y + 3, NY)
    for a in range(2):
        add_core(a, 2)
        go_on(remote(q.at[a, y2], s1.at[a], ys.at[a, 0], yr.at[a, 0], "expert", (y_up, y_down)[a]))
    for dy in (1, 3):
        for a in range(2):
            add_core(a, dy)
    go_on(remote(q.at[1, y1], fy.at[1, 0], ys.at[1, 1], yr.at[1, 1], "expert", y_up))
    go_on(remote(q.at[0, y3], fy.at[0, 1], ys.at[0, 2], yr.at[0, 2], "expert", y_down))
    for a in range(2):
        near = (y1, y3)[a]
        remote(s1.at[a], s1.at[a], ys.at[a, 0], yr.at[a, 0], "expert", twin).wait_recv()

        @pl.loop(0, NZ)
        def _(k):
            s1[a, k] = (q[a, near, k].astype(F32) + s1[a, k].astype(F32)).astype(BF16)

        go_on(remote(s1.at[a], fy.at[a, a], ys.at[a, 1 + a], yr.at[a, 1 + a], "expert",
                     (y_up, y_down)[a]))
    for a in range(2):
        add_core(a, 0)
        for side in range(2):
            remote(fy.at[a, side], fy.at[a, side], ys.at[a, 0], yr.at[a, 1 + side], "expert",
                   twin).wait_recv()

        @pl.loop(0, NZ)
        def _(k):
            r[a, k] = (q[a, y, k].astype(F32) + fy[a, 0, k].astype(F32)
                       + fy[a, 1, k].astype(F32)).astype(BF16)

    h2, h1, h3 = lax.rem(zh + 2, NZ), lax.rem(zh + 1, NZ), lax.rem(zh + 3, NZ)
    for a in range(2):
        go_on(remote(r.at[a, h2], s1z.at[a], zs.at[a, 0], zr.at[a, 0], "expert", (z_up, z_down)[a]))
    go_on(remote(r.at[1, h1], fz.at[1, 0], zs.at[1, 1], zr.at[1, 1], "expert", z_up))
    go_on(remote(r.at[0, h3], fz.at[0, 1], zs.at[0, 2], zr.at[0, 2], "expert", z_down))
    for a in range(2):
        near = (h1, h3)[a]
        remote(s1z.at[a], s1z.at[a], zs.at[a, 0], zr.at[a, 0], "expert", twin).wait_recv()
        r2[a] = (r[a, near].astype(F32) + s1z[a].astype(F32)).astype(BF16)
        go_on(remote(r2.at[a], fz.at[a, a], zs.at[a, 1 + a], zr.at[a, 1 + a], "expert",
                     (z_up, z_down)[a]))
    outs = (mo, no)
    for a in range(2):
        for side in range(2):
            remote(fz.at[a, side], fz.at[a, side], zs.at[a, 0], zr.at[a, 1 + side], "expert",
                   twin).wait_recv()
        whole = r[a, zh].astype(F32) + fz[a, 0].astype(F32) + fz[a, 1].astype(F32)
        outs[a][...] = whole.astype(outs[a].dtype)

    @pl.loop(1, total)
    def _(i):
        source = lax.rem(j + i, total)
        remote(gp, go.at[source], gs.at[i], gr.at[source], "expert", twin).wait_recv()
        pull_copy(i).wait_send()

    keep.wait()
    for copy in sent:
        copy.wait_send()


def give_back(pm, pn, gp):
    d = pm.shape[-1]
    total = 2 * NY * NZ
    dma = pltpu.SemaphoreType.DMA
    return pl.pallas_call(
        return_kernel,
        out_shape=[
            jax.ShapeDtypeStruct((8, d), BF16),
            jax.ShapeDtypeStruct((8, d), F32),
            jax.ShapeDtypeStruct((total, *gp.shape), F32),
        ],
        in_specs=[VMEM] * 3,
        out_specs=[VMEM] * 3,
        scratch_shapes=[
            pltpu.VMEM((2, NY, NZ, 8, d), BF16),
            pltpu.VMEM((2, NY, NZ, 8, d), BF16),
            pltpu.VMEM((2, NZ, 8, d), BF16),
            pltpu.VMEM((2, 2, NZ, 8, d), BF16),
            pltpu.VMEM((2, NZ, 8, d), BF16),
            pltpu.VMEM((2, 8, d), BF16),
            pltpu.VMEM((2, 2, 8, d), BF16),
            pltpu.VMEM((2, 8, d), BF16),
            dma((2, NY)), dma((2, NY)), dma((2, 3)), dma((2, 3)), dma((2, 3)), dma((2, 3)),
            dma((total,)), dma((total,)), dma,
        ],
        compiler_params=pltpu.CompilerParams(collective_id=1, has_side_effects=True),
        name="group_return",
    )(pm, pn, gp)


def reduce_kernel(w0, w1, w2, g, o0, o1, o2, go, s1, fx, aug, u, zbuf, gx, gsum, gz, gtot,
                  xs, xr, zs, zr, gs, gr, gl):
    dev = lax.axis_index("dp")
    x, zl = lax.div(dev, 4), lax.rem(dev, 4)

    def at(xx, zz):
        return lax.rem(xx, 4) * 4 + lax.rem(zz, 4)

    x_up, x_down = at(x + 1, zl), at(x + 3, zl)
    greet("dp", [at(x + d, zl) for d in (1, 2, 3)] + [at(x, zl + d) for d in (1, 2, 3)])
    ws, outs = (w0, w1, w2), (o0, o1, o2)
    x1, x2, x3 = lax.rem(x + 1, 4), lax.rem(x + 2, 4), lax.rem(x + 3, 4)
    lo, hi = pl.ds(0, 2), pl.ds(2, 2)
    cols = gx.shape[-1]
    sent = []

    def go_on(copy):
        copy.start()
        sent.append(copy)

    def landed(ref, sem):
        remote(ref, ref, sem, sem, "dp", x_up).wait_recv()

    def first(p):
        go_on(remote(ws[p].at[x2, lo], s1.at[p, 0], xs.at[p, 0], xr.at[p, 0], "dp", x_up))
        go_on(remote(ws[p].at[x2, hi], s1.at[p, 1], xs.at[p, 1], xr.at[p, 1], "dp", x_down))

    def plain(p):
        go_on(remote(ws[p].at[x1, hi], fx.at[p, 0, 1], xs.at[p, 2], xr.at[p, 2], "dp", x_up))
        go_on(remote(ws[p].at[x3, lo], fx.at[p, 1, 0], xs.at[p, 3], xr.at[p, 3], "dp", x_down))

    def passed(p):
        for h in range(2):
            landed(s1.at[p, h], xr.at[p, h])
            near = (x1, x3)[h]
            for k in range(2):
                aug[p, h, k] = (ws[p][near, 2 * h + k].astype(F32)
                                + s1[p, h, k].astype(F32)).astype(BF16)
            go_on(remote(aug.at[p, h], fx.at[p, h, h], xs.at[p, 4 + h], xr.at[p, 4 + h], "dp",
                         (x_up, x_down)[h]))

    def lane(xx):
        return pl.ds(pl.multiple_of(lax.rem(xx, 4) * cols, cols), cols)

    def across(p):
        for i in (2, 3, 4, 5):
            ref = (fx.at[p, 0, 1], fx.at[p, 1, 0], fx.at[p, 0, 0], fx.at[p, 1, 1])[i - 2]
            landed(ref, xr.at[p, i])
        for k in range(4):
            u[p, k] = (ws[p][x, k].astype(F32) + fx[p, 0, k // 2, k % 2].astype(F32)
                       + fx[p, 1, k // 2, k % 2].astype(F32)).astype(BF16)
        for d in (2, 1, 3):
            go_on(remote(u.at[p, lax.rem(zl + d, 4)], zbuf.at[p, d - 1], zs.at[p, d - 1],
                         zr.at[p, d - 1], "dp", at(x, zl + d)))

    first(0)
    plain(0)
    for d in (1, 2, 3):
        go_on(remote(g.at[:, lane(x + d)], gx.at[d - 1], gs.at[0, d - 1], gr.at[0, d - 1], "dp",
                     at(x + d, zl)))
    first(1)
    passed(0)
    plain(1)
    first(2)
    for d in range(3):
        landed(gx.at[d], gr.at[0, d])
    gsum[...] = g[:, lane(x)] + gx[0] + gx[1] + gx[2]
    for d in (1, 2, 3):
        go_on(remote(gsum, gz.at[d - 1], gs.at[1, d - 1], gr.at[1, d - 1], "dp", at(x, zl + d)))
    passed(1)
    plain(2)
    across(0)
    for d in range(3):
        landed(gz.at[d], gr.at[1, d])
    gtot[...] = gsum[...] + gz[0] + gz[1] + gz[2]
    for d in (1, 2, 3):
        go_on(remote(gtot, go.at[:, lane(x)], gs.at[2, d - 1], gr.at[2, d - 1], "dp", at(x + d, zl)))
    own = pltpu.make_async_copy(gtot, go.at[:, lane(x)], gl)
    own.start()
    passed(2)
    across(1)
    across(2)
    for p in range(3):
        for d in range(3):
            landed(zbuf.at[p, d], zr.at[p, d])
        outs[p][...] = (u[p, zl].astype(F32) + zbuf[p, 0].astype(F32)
                        + zbuf[p, 1].astype(F32) + zbuf[p, 2].astype(F32))
    for d in range(3):
        landed(go.at[:, lane(x + 3 - d)], gr.at[2, d])
    own.wait()
    for copy in sent:
        copy.wait_send()


def reduce_weights(dws, g):
    rows, f = dws[0].shape
    n = rows // 16
    ws = [w.reshape(4, 4, n, f) for w in dws]
    cols = g.shape[1] // 4
    dma = pltpu.SemaphoreType.DMA
    return pl.pallas_call(
        reduce_kernel,
        out_shape=[jax.ShapeDtypeStruct((n, f), F32)] * 3 + [jax.ShapeDtypeStruct(g.shape, F32)],
        in_specs=[VMEM] * 4,
        out_specs=[VMEM] * 4,
        scratch_shapes=[
            pltpu.VMEM((3, 2, 2, n, f), BF16),
            pltpu.VMEM((3, 2, 2, 2, n, f), BF16),
            pltpu.VMEM((3, 2, 2, n, f), BF16),
            pltpu.VMEM((3, 4, n, f), BF16),
            pltpu.VMEM((3, 3, n, f), BF16),
            pltpu.VMEM((3, 8, cols), F32),
            pltpu.VMEM((8, cols), F32),
            pltpu.VMEM((3, 8, cols), F32),
            pltpu.VMEM((8, cols), F32),
            dma((3, 6)), dma((3, 6)), dma((3, 3)), dma((3, 3)), dma((3, 3)), dma((3, 3)), dma,
        ],
        compiler_params=pltpu.CompilerParams(collective_id=2, has_side_effects=True),
        name="weight_reduce",
    )(*ws, g)


def dot(a, b, contract):
    return lax.dot_general(a, b, (contract, ((), ())), preferred_element_type=F32)


def local(tokens, routes, router, w_gate, w_up, w_down, cotangent):
    d = tokens.shape[1]
    experts = router.shape[1]
    f = w_gate.shape[1]
    highest = lax.Precision.HIGHEST
    j = lax.axis_index("expert")
    lanes = jnp.arange(128, dtype=jnp.int32)
    mark = jnp.sum((routes[:, :, None] == lanes).astype(F32), axis=1)
    xg, cg, mg = gather(tokens, cotangent, mark)
    x = xg.reshape(-1, d)
    c = cg.reshape(-1, d)
    mask = mg.reshape(-1, 128)[:, :experts]
    rows = x.shape[0]
    logits = jnp.dot(x.astype(F32), router, precision=highest)
    affinity = jax.nn.sigmoid(logits)
    denominator = jnp.sum(affinity * mask, axis=1, keepdims=True)
    gates = mask * affinity / denominator
    mine = (jnp.arange(experts) == j // 4).astype(F32)
    gate = jnp.sum(gates * mine, axis=1, keepdims=True)
    gate_pre = dot(x, w_gate, ((1,), (0,)))
    up_pre = dot(x, w_up, ((1,), (0,)))
    pull = dot(c, w_down, ((1,), (0,)))
    sigma = jax.nn.sigmoid(gate_pre)
    silu = gate_pre * sigma
    hidden = silu * up_pre
    scaled = (gate * hidden).astype(BF16)
    gate_pull = jnp.sum(hidden * pull, axis=1)
    hidden_grad = gate * pull
    gate_grad = (hidden_grad * up_pre * sigma * (1.0 + gate_pre * (1.0 - sigma))).astype(BF16)
    up_grad = (hidden_grad * silu).astype(BF16)
    out_part = dot(scaled, w_down, ((1,), (1,))).astype(BF16)
    in_part = (dot(gate_grad, w_gate, ((1,), (1,))) + dot(up_grad, w_up, ((1,), (1,)))).astype(BF16)
    dws = [
        dot(x, gate_grad, ((0,), (0,))).astype(BF16),
        dot(x, up_grad, ((0,), (0,))).astype(BF16),
        dot(c, scaled, ((0,), (0,))).astype(BF16),
    ]
    split = (NY, NZ, 2, 8, d)
    mixed, input_sum, pulls = give_back(
        out_part.reshape(split), in_part.reshape(split), gate_pull.reshape(1, rows)
    )
    full_pull = jnp.sum(pulls.reshape(experts, -1, rows), axis=1).T
    mean_pull = jnp.sum(gates * full_pull, axis=1, keepdims=True)
    logit_grad = mask * (full_pull - mean_pull) / denominator * affinity * (1.0 - affinity)
    router_part = lax.dot_general(
        logit_grad, x.astype(F32), (((0,), (0,)), ((), ())), precision=highest
    )
    own = lax.dynamic_slice(logit_grad, (j * 8, 0), (8, experts))
    router_back = lax.dot_general(own, router, (((1,), (1,)), ((), ())), precision=highest)
    grad_tokens = (input_sum + router_back).astype(BF16)
    grad_gate, grad_up, grad_down, grad_router = reduce_weights(dws, router_part)
    return (mixed, grad_tokens, grad_router.T, grad_gate, grad_up, grad_down)


def solution(mesh):
    return jax.shard_map(
        local,
        mesh=mesh,
        in_specs=(
            P(("dp", "expert"), None),
            P(("dp", "expert"), None),
            P(),
            P(None, "expert"),
            P(None, "expert"),
            P(None, "expert"),
            P(("dp", "expert"), None),
        ),
        out_specs=(
            P(("dp", "expert"), None),
            P(("dp", "expert"), None),
            P(),
            P("dp", "expert"),
            P("dp", "expert"),
            P("dp", "expert"),
        ),
        check_vma=False,
    )
```

```python
import jax
import jax.numpy as jnp
from jax import lax
from jax.experimental import pallas as pl
from jax.experimental.pallas import tpu as pltpu
from jax.sharding import PartitionSpec as P

NY = 4
NZ = 4
NX = 4
NL = 4
GROUP = 2 * NY * NZ
MESH = pl.DeviceIdType.MESH
VMEM = pl.BlockSpec(memory_space=pltpu.VMEM)
ANY = pl.BlockSpec(memory_space=pl.ANY)
F32 = jnp.float32
BF16 = jnp.bfloat16


def member(y, zh, core):
    return (lax.rem(y, NY) * NZ + lax.rem(zh, NZ)) * 2 + core


def dot(a, b, contract):
    return lax.dot_general(a, b, (contract, ((), ())), preferred_element_type=F32)


def thirds(a):
    one = a.astype(BF16).astype(F32)
    two = (a - one).astype(BF16).astype(F32)
    return jnp.concatenate([one, two, a - one - two], axis=0).astype(BF16)


def regroup(a):
    n = a.shape[0] // 3
    return a[:n] + a[n : 2 * n] + a[2 * n :]


def layer_kernel(x_ref, c_ref, m_ref, rt, wg_hbm, wu_hbm, wd_hbm,
                 zo, mo, no, go,
                 xg, cg, mg, pg, prow, wts, gate_pre, up_pre, pull, hs, dg, du, lt,
                 part, cbuf, q, s1, fy, r, s1z, fz, r2,
                 dw, s1x, fx, aug, gx, gsum,
                 wsem, as_, ar, al, ms, mr, ps, pr, ml, cs, cr, ys, yr, zs, zr,
                 xs, xr, us, ur, gs, gr, gl):
    j = lax.axis_index("expert")
    core = lax.rem(j, 2)
    zh = lax.rem(lax.div(j, 2), NZ)
    y = lax.div(j, 2 * NZ)
    dev = lax.axis_index("dp")
    x, zl = lax.div(dev, NL), lax.rem(dev, NL)
    d = x_ref.shape[1]
    rows = GROUP * 8

    def place(xx, zz):
        return lax.rem(xx, NX) * NL + lax.rem(zz, NL)

    def at(dy, dz):
        return member(y + dy, zh + dz, core)

    twin = member(y, zh, 1 - core)
    z_up, z_down, y_up, y_down = at(0, 1), at(0, 3), at(1, 0), at(3, 0)
    x_up, x_down = place(x + 1, zl), place(x + 3, zl)

    loads = [pltpu.make_async_copy(w, wts.at[i], wsem.at[i])
             for i, w in enumerate((wg_hbm, wu_hbm, wd_hbm))]
    for copy in loads:
        copy.start()

    barrier = pltpu.get_barrier_semaphore()
    near = [at(0, 1), at(0, 2), at(0, 3), at(1, 0), at(2, 0), at(3, 0), twin]
    wide = [place(x + k, zl) for k in (1, 2, 3)] + [place(x, zl + k) for k in (1, 2, 3)]
    for peer in near:
        pl.semaphore_signal(barrier, inc=1, device_id={"expert": peer}, device_id_type=MESH)
    for peer in wide:
        pl.semaphore_signal(barrier, inc=1, device_id={"dp": peer}, device_id_type=MESH)
    pl.semaphore_wait(barrier, len(near) + len(wide))

    sent = []

    def remote(src, dst, send_sem, recv_sem, axis, target):
        return pltpu.make_async_remote_copy(
            src_ref=src, dst_ref=dst, send_sem=send_sem, recv_sem=recv_sem,
            device_id={axis: target}, device_id_type=MESH,
        )

    def go_on(*args):
        copy = remote(*args)
        copy.start()
        sent.append(copy)

    def landed(ref, sem):
        remote(ref, ref, sem, sem, "expert", twin).wait_recv()

    ins, outs = (x_ref, c_ref), (xg, cg)
    used = [0, 0]

    def send(a, block, target, own=False):
        go_on(ins[a] if own else outs[a].at[block], outs[a].at[block],
              as_.at[a, used[a]], ar.at[a, block], "expert", target)
        used[a] += 1

    def arrive(a, block):
        landed(outs[a].at[block], ar.at[a, block])

    def spread(a, dz):
        for target in (y_up, y_down, twin):
            send(a, at(0, dz), target)

    def side(dz):
        arrive(0, at(3, dz))
        send(0, at(3, dz), y_up)
        send(0, at(3, dz), twin)
        arrive(1, at(1, dz))
        send(1, at(1, dz), y_down)
        send(1, at(1, dz), twin)
        arrive(0, at(1, dz))
        send(0, at(1, dz), twin)
        arrive(1, at(3, dz))
        send(1, at(3, dz), twin)

    def far(dz):
        for a in range(2):
            arrive(a, at(2, dz))
            send(a, at(2, dz), twin)

    class Small:
        def __init__(self, src, out, ssem, rsem, local):
            self.src, self.out, self.ssem, self.rsem, self.used = src, out, ssem, rsem, 0
            self.keep = pltpu.make_async_copy(src, out.at[j], local)

        def send(self, block, target, own=False):
            go_on(self.src if own else self.out.at[block], self.out.at[block],
                  self.ssem.at[self.used], self.rsem.at[block], "expert", target)
            self.used += 1

        def arrive(self, block):
            landed(self.out.at[block], self.rsem.at[block])

        def first(self):
            for k in (1, 2, 3):
                self.send(j, at(0, k), True)
            for k in (1, 2, 3):
                self.send(j, at(k, 0), True)
            self.send(j, twin, True)
            self.keep.start()

        def second(self):
            for k in (1, 3, 2):
                self.arrive(at(0, k))
                for target in (y_up, at(2, 0), y_down, twin):
                    self.send(at(0, k), target)

        def third(self):
            for dz in (0, 1, 3, 2):
                for dy in (1, 3, 2):
                    self.arrive(at(dy, dz))
                    self.send(at(dy, dz), twin)

        def last(self):
            self.keep.wait()
            for i in range(NY * NZ):
                self.arrive(2 * i + 1 - core)

    marks = Small(m_ref, mg, ms, mr, ml.at[0])
    pulls = Small(prow, pg, ps, pr, ml.at[1])

    for a in range(2):
        send(a, j, z_up, True)
        send(a, j, z_down, True)
    marks.first()
    for a in range(2):
        send(a, j, y_up, True)
        send(a, j, y_down, True)
        send(a, j, twin, True)
    held = [pltpu.make_async_copy(ins[a], outs[a].at[j], al.at[a]) for a in range(2)]
    for copy in held:
        copy.start()
    arrive(0, at(0, 3))
    send(0, at(0, 3), z_up)
    spread(0, 3)
    arrive(0, at(0, 1))
    spread(0, 1)
    arrive(1, at(0, 1))
    send(1, at(0, 1), z_down)
    spread(1, 1)
    arrive(1, at(0, 3))
    spread(1, 3)
    side(0)
    marks.second()
    far(0)
    side(3)
    side(1)
    arrive(0, at(0, 2))
    spread(0, 2)
    arrive(1, at(0, 2))
    spread(1, 2)
    marks.third()
    far(3)
    far(1)
    side(2)
    far(2)
    marks.last()
    for copy in loads + held:
        copy.wait()
    for i in range(NY * NZ):
        arrive(0, 2 * i + 1 - core)

    xv, cv = xg.reshape(rows, d), cg.reshape(rows, d)
    mask = jnp.transpose(mg.reshape(rows, 128)[...])[:8]
    logits = regroup(dot(thirds(rt[...]), xv[...], ((1,), (1,))))
    affinity = jax.nn.sigmoid(logits)
    denominator = jnp.sum(affinity * mask, axis=0, keepdims=True)
    gates = mask * affinity / denominator
    wide_gates = jnp.transpose(jnp.concatenate([gates, jnp.zeros((120, rows), F32)], axis=0))
    mine = lax.broadcasted_iota(jnp.int32, wide_gates.shape, 1) == lax.div(j, 4)
    gate = jnp.sum(jnp.where(mine, wide_gates, 0.0), axis=1, keepdims=True)
    gate_pre[...] = dot(xv[...], wts[0], ((1,), (0,)))
    up_pre[...] = dot(xv[...], wts[1], ((1,), (0,)))
    for i in range(NY * NZ):
        arrive(1, 2 * i + 1 - core)
    pull[...] = dot(cv[...], wts[2], ((1,), (0,)))
    sigma = jax.nn.sigmoid(gate_pre[...])
    silu = gate_pre[...] * sigma
    hidden = silu * up_pre[...]
    hs[...] = (gate * hidden).astype(BF16)
    prow[...] = jnp.sum(jnp.transpose(hidden * pull[...]), axis=0, keepdims=True)
    hidden_grad = gate * pull[...]
    dg[...] = (hidden_grad * up_pre[...] * sigma
               * (1.0 + gate_pre[...] * (1.0 - sigma))).astype(BF16)
    du[...] = (hidden_grad * silu).astype(BF16)

    x1, x2, x3 = lax.rem(x + 1, NX), lax.rem(x + 2, NX), lax.rem(x + 3, NX)
    low, high = pl.ds(0, 2), pl.ds(2, 2)
    chunk = d // NX
    cols = chunk

    def weight_part(p, xx):
        left = xv if p else cv
        span = pl.ds(pl.multiple_of(xx * chunk, chunk), chunk)
        value = dot(left[:, span], (hs, dg, du)[p][...], ((0,), (0,)))
        dw[p, xx] = value.astype(BF16).reshape(dw.shape[2:])

    def first(p):
        weight_part(p, x2)
        go_on(dw.at[p, x2, low], s1x.at[p, 0], xs.at[p, 0], xr.at[p, 0], "dp", x_up)
        go_on(dw.at[p, x2, high], s1x.at[p, 1], xs.at[p, 1], xr.at[p, 1], "dp", x_down)

    def plain(p):
        weight_part(p, x1)
        go_on(dw.at[p, x1, high], fx.at[p, 0, 1], xs.at[p, 2], xr.at[p, 2], "dp", x_up)
        weight_part(p, x3)
        go_on(dw.at[p, x3, low], fx.at[p, 1, 0], xs.at[p, 3], xr.at[p, 3], "dp", x_down)

    def passed(p):
        for h in range(2):
            landed(s1x.at[p, h], xr.at[p, h])
            for k in range(2):
                aug[p, h, k] = (dw[p, (x1, x3)[h], 2 * h + k].astype(F32)
                                + s1x[p, h, k].astype(F32)).astype(BF16)
            go_on(aug.at[p, h], fx.at[p, h, h], xs.at[p, 4 + h], xr.at[p, 4 + h], "dp",
                  (x_up, x_down)[h])

    def across(p):
        for i in (2, 3, 4, 5):
            side_, half = ((0, 1), (1, 0), (0, 0), (1, 1))[i - 2]
            landed(fx.at[p, side_, half], xr.at[p, i])
        for k in range(NL):
            dw[p, x, k] = (dw[p, x, k].astype(F32) + fx[p, 0, k // 2, k % 2].astype(F32)
                           + fx[p, 1, k // 2, k % 2].astype(F32)).astype(BF16)
        for k in (2, 1, 3):
            go_on(dw.at[p, x, lax.rem(zl + k, NL)], zo.at[p, k], us.at[p, k - 1],
                  ur.at[p, k - 1], "dp", place(x, zl + k))
        zo[p, 0] = dw[p, x, zl]

    def start_core(a):
        for dy in (2, 1, 3, 0):
            yy = lax.rem(y + dy, NY)
            go_on(part.at[a, yy, :, 1 - core], cbuf.at[a, yy], cs.at[a, dy], cr.at[a, yy],
                  "expert", twin)

    def add_core(a, dy):
        yy = lax.rem(y + dy, NY)
        landed(cbuf.at[a, yy], cr.at[a, yy])

        @pl.loop(0, NZ)
        def _(k):
            q[a, yy, k] = (part[a, yy, k, core].astype(F32)
                           + cbuf[a, yy, k].astype(F32)).astype(BF16)

    y1, y2, y3 = lax.rem(y + 1, NY), lax.rem(y + 2, NY), lax.rem(y + 3, NY)

    def y_first():
        for a in range(2):
            add_core(a, 2)
            go_on(q.at[a, y2], s1.at[a], ys.at[a, 0], yr.at[a, 0], "expert", (y_up, y_down)[a])
        for dy in (1, 3):
            for a in range(2):
                add_core(a, dy)
        go_on(q.at[1, y1], fy.at[1, 0], ys.at[1, 1], yr.at[1, 1], "expert", y_up)
        go_on(q.at[0, y3], fy.at[0, 1], ys.at[0, 2], yr.at[0, 2], "expert", y_down)

    def y_second():
        for a in range(2):
            landed(s1.at[a], yr.at[a, 0])

            @pl.loop(0, NZ)
            def _(k):
                s1[a, k] = (q[a, (y1, y3)[a], k].astype(F32) + s1[a, k].astype(F32)).astype(BF16)

            go_on(s1.at[a], fy.at[a, a], ys.at[a, 1 + a], yr.at[a, 1 + a], "expert",
                  (y_up, y_down)[a])
        for a in range(2):
            add_core(a, 0)

    h1, h2, h3 = lax.rem(zh + 1, NZ), lax.rem(zh + 2, NZ), lax.rem(zh + 3, NZ)

    def z_first():
        for a in range(2):
            for s in range(2):
                landed(fy.at[a, s], yr.at[a, 1 + s])

            @pl.loop(0, NZ)
            def _(k):
                r[a, k] = (q[a, y, k].astype(F32) + fy[a, 0, k].astype(F32)
                           + fy[a, 1, k].astype(F32)).astype(BF16)

            go_on(r.at[a, h2], s1z.at[a], zs.at[a, 0], zr.at[a, 0], "expert", (z_up, z_down)[a])
        go_on(r.at[1, h1], fz.at[1, 0], zs.at[1, 1], zr.at[1, 1], "expert", z_up)
        go_on(r.at[0, h3], fz.at[0, 1], zs.at[0, 2], zr.at[0, 2], "expert", z_down)

    def z_second():
        for a in range(2):
            landed(s1z.at[a], zr.at[a, 0])
            r2[a] = (r[a, (h1, h3)[a]].astype(F32) + s1z[a].astype(F32)).astype(BF16)
            go_on(r2.at[a], fz.at[a, a], zs.at[a, 1 + a], zr.at[a, 1 + a], "expert",
                  (z_up, z_down)[a])

    def z_third(a):
        for s in range(2):
            landed(fz.at[a, s], zr.at[a, 1 + s])
        return r[a, zh].astype(F32) + fz[a, 0].astype(F32) + fz[a, 1].astype(F32)

    def lane(xx):
        return pl.ds(pl.multiple_of(lax.rem(xx, NX) * cols, cols), cols)

    def router_first():
        pulls.last()
        sums = []
        for e in range(8):
            sums.append(pg[4 * e] + pg[4 * e + 1] + pg[4 * e + 2] + pg[4 * e + 3])
        full = jnp.concatenate(sums, axis=0)
        mean = jnp.sum(gates * full, axis=0, keepdims=True)
        lt[...] = mask * (full - mean) / denominator * affinity * (1.0 - affinity)
        value = regroup(dot(thirds(lt[...]), xv[...], ((1,), (0,))))
        for k in range(NX):
            gx[k] = value[:, k * cols : (k + 1) * cols]
        for k in (1, 2, 3):
            go_on(gx.at[lax.rem(x + k, NX)], gx.at[NX + k - 1], gs.at[0, k - 1],
                  gr.at[0, k - 1], "dp", place(x + k, zl))

    def router_second():
        for k in range(3):
            landed(gx.at[NX + k], gr.at[0, k])
        gsum[...] = gx[x] + gx[NX] + gx[NX + 1] + gx[NX + 2]
        for k in (1, 2, 3):
            go_on(gsum, go.at[zl, :, lane(x)], gs.at[1, k - 1], gr.at[1, k - 1], "dp",
                  place(x, zl + k))
        keep = pltpu.make_async_copy(gsum, go.at[zl, :, lane(x)], gl)
        keep.start()
        keep.wait()

    def router_third():
        for k in (1, 2, 3):
            landed(go.at[lax.rem(zl + NL - k, NL), :, lane(x)], gr.at[1, k - 1])
        for k in (1, 2, 3):
            go_on(go.at[:, :, lane(x)], go.at[:, :, lane(x)], gs.at[2, k - 1], gr.at[2, k - 1],
                  "dp", place(x + k, zl))

    def router_last():
        for k in (1, 2, 3):
            landed(go.at[:, :, lane(x + NX - k)], gr.at[2, k - 1])

    first(0)
    pulls.first()
    plain(0)
    part.reshape(2, rows, d)[0] = dot(hs[...], wts[2], ((1,), (1,))).astype(BF16)
    start_core(0)
    part.reshape(2, rows, d)[1] = (dot(dg[...], wts[0], ((1,), (1,)))
                                   + dot(du[...], wts[1], ((1,), (1,)))).astype(BF16)
    start_core(1)
    first(1)
    y_first()
    passed(0)
    plain(1)
    y_second()
    first(2)
    pulls.second()
    passed(1)
    plain(2)
    weight_part(0, x)
    z_first()
    pulls.third()
    across(0)
    router_first()
    weight_part(1, x)
    weight_part(2, x)
    z_second()
    passed(2)
    router_second()
    across(1)
    mo[...] = z_third(0)
    total = z_third(1)
    ours = lax.broadcasted_iota(jnp.int32, (8, rows), 0) + 8 * j
    pick = lax.broadcasted_iota(jnp.int32, (8, rows), 1) == ours
    for e in range(8):
        weight = jnp.sum(jnp.where(pick, lt[e : e + 1, :], 0.0), axis=1, keepdims=True)
        total = total + weight * rt[e : e + 1, :]
    no[...] = total
    router_third()
    across(2)
    router_last()
    for p in range(3):
        for k in range(3):
            landed(zo.at[p, k + 1], ur.at[p, k])
    for copy in sent:
        copy.wait_send()


def layer(tokens, cotangent, mark, router_t, w_gate, w_up, w_down):
    d = tokens.shape[1]
    f = w_gate.shape[1]
    rows = GROUP * 8
    n = d // (NX * NL)
    cols = d // NX
    dma = pltpu.SemaphoreType.DMA
    return pl.pallas_call(
        layer_kernel,
        out_shape=[
            jax.ShapeDtypeStruct((3, NL, n, f), BF16),
            jax.ShapeDtypeStruct((8, d), F32),
            jax.ShapeDtypeStruct((8, d), F32),
            jax.ShapeDtypeStruct((NL, 8, d), F32),
        ],
        in_specs=[VMEM] * 4 + [ANY] * 3,
        out_specs=[VMEM] * 4,
        scratch_shapes=[
            pltpu.VMEM((GROUP, 8, d), BF16),
            pltpu.VMEM((GROUP, 8, d), BF16),
            pltpu.VMEM((GROUP, 8, 128), F32),
            pltpu.VMEM((GROUP, 1, rows), F32),
            pltpu.VMEM((1, rows), F32),
            pltpu.VMEM((3, d, f), BF16),
            pltpu.VMEM((rows, f), F32),
            pltpu.VMEM((rows, f), F32),
            pltpu.VMEM((rows, f), F32),
            pltpu.VMEM((rows, f), BF16),
            pltpu.VMEM((rows, f), BF16),
            pltpu.VMEM((rows, f), BF16),
            pltpu.VMEM((8, rows), F32),
            pltpu.VMEM((2, NY, NZ, 2, 8, d), BF16),
            pltpu.VMEM((2, NY, NZ, 8, d), BF16),
            pltpu.VMEM((2, NY, NZ, 8, d), BF16),
            pltpu.VMEM((2, NZ, 8, d), BF16),
            pltpu.VMEM((2, 2, NZ, 8, d), BF16),
            pltpu.VMEM((2, NZ, 8, d), BF16),
            pltpu.VMEM((2, 8, d), BF16),
            pltpu.VMEM((2, 2, 8, d), BF16),
            pltpu.VMEM((2, 8, d), BF16),
            pltpu.VMEM((3, NX, NL, n, f), BF16),
            pltpu.VMEM((3, 2, 2, n, f), BF16),
            pltpu.VMEM((3, 2, 2, 2, n, f), BF16),
            pltpu.VMEM((3, 2, 2, n, f), BF16),
            pltpu.VMEM((NX + 3, 8, cols), F32),
            pltpu.VMEM((8, cols), F32),
            dma((3,)), dma((2, 31)), dma((2, GROUP)), dma((2,)),
            dma((31,)), dma((GROUP,)), dma((31,)), dma((GROUP,)), dma((2,)),
            dma((2, NY)), dma((2, NY)), dma((2, 3)), dma((2, 3)), dma((2, 3)), dma((2, 3)),
            dma((3, 6)), dma((3, 6)), dma((3, 3)), dma((3, 3)), dma((3, 3)), dma((3, 3)), dma,
        ],
        compiler_params=pltpu.CompilerParams(collective_id=0, has_side_effects=True),
        name="moe_layer",
    )(tokens, cotangent, mark, router_t, w_gate, w_up, w_down)


def finish_kernel(z, m, t, g, mo, to, go, o0, o1, o2):
    mo[...] = m[...].astype(BF16)
    to[...] = t[...].astype(BF16)
    go[...] = g[0] + g[1] + g[2] + g[3]
    for out, p in ((o2, 0), (o0, 1), (o1, 2)):
        out[...] = (z[p, 0].astype(F32) + z[p, 1].astype(F32)
                    + z[p, 2].astype(F32) + z[p, 3].astype(F32))


def finish(z, m, t, g):
    grad = jax.ShapeDtypeStruct(z.shape[2:], F32)
    token = jax.ShapeDtypeStruct(m.shape, BF16)
    return pl.pallas_call(
        finish_kernel,
        out_shape=[token, token, jax.ShapeDtypeStruct(g.shape[1:], F32), grad, grad, grad],
        in_specs=[VMEM] * 4,
        out_specs=[VMEM] * 6,
        name="finish",
    )(z, m, t, g)


def local(tokens, routes, router, w_gate, w_up, w_down, cotangent):
    lanes = jnp.arange(128, dtype=jnp.int32)
    mark = jnp.sum((routes[:, :, None] == lanes).astype(F32), axis=1)
    parts = layer(tokens, cotangent, mark, router.T, w_gate, w_up, w_down)
    mixed, grad_tokens, grad_router, grad_gate, grad_up, grad_down = finish(*parts)
    return (mixed, grad_tokens, grad_router.T, grad_gate, grad_up, grad_down)


def solution(mesh):
    return jax.shard_map(
        local,
        mesh=mesh,
        in_specs=(
            P(("dp", "expert"), None),
            P(("dp", "expert"), None),
            P(),
            P(None, "expert"),
            P(None, "expert"),
            P(None, "expert"),
            P(("dp", "expert"), None),
        ),
        out_specs=(
            P(("dp", "expert"), None),
            P(("dp", "expert"), None),
            P(),
            P("dp", "expert"),
            P("dp", "expert"),
            P("dp", "expert"),
        ),
        check_vma=False,
    )
```

```python
import jax
import jax.numpy as jnp
from jax import lax
from jax.experimental import pallas as pl
from jax.experimental.pallas import tpu as pltpu
from jax.sharding import PartitionSpec as P

NY = 4
NZ = 4
NX = 4
NL = 4
GROUP = 2 * NY * NZ
MESH = pl.DeviceIdType.MESH
VMEM = pl.BlockSpec(memory_space=pltpu.VMEM)
ANY = pl.BlockSpec(memory_space=pl.ANY)
F32 = jnp.float32
BF16 = jnp.bfloat16


def member(y, zh, core):
    return (lax.rem(y, NY) * NZ + lax.rem(zh, NZ)) * 2 + core


def dot(a, b, contract):
    return lax.dot_general(a, b, (contract, ((), ())), preferred_element_type=F32)


def thirds(a):
    one = a.astype(BF16).astype(F32)
    two = (a - one).astype(BF16).astype(F32)
    return jnp.concatenate([one, two, a - one - two], axis=0).astype(BF16)


def regroup(a):
    n = a.shape[0] // 3
    return a[:n] + a[n : 2 * n] + a[2 * n :]


def layer_kernel(x_hbm, c_hbm, routes_hbm, rt_hbm, wg_hbm, wu_hbm, wd_hbm,
                 wo_hbm, to_hbm, go_hbm,
                 x_ref, c_ref, routes_ref, rt, zo, go, wo, to, gout,
                 xg, cg, mg, m_ref, pg, prow, wts, gate_pre, up_pre, pull, acts, lt,
                 part, cbuf, q, s1, fy, r, s1z, fz, r2,
                 dw, slices, aid, gx, gsum,
                 isem, osem, wsem, as_, ar, al, ms, mr, ps, pr, ml, cs, cr, ys, yr, zs, zr,
                 es, er, ts, tr, xs, xr, vs, vr, us, ur, hs_, hr, gs, gr, gl):
    j = lax.axis_index("expert")
    core = lax.rem(j, 2)
    zh = lax.rem(lax.div(j, 2), NZ)
    y = lax.div(j, 2 * NZ)
    dev = lax.axis_index("dp")
    x, zl = lax.div(dev, NL), lax.rem(dev, NL)
    d = x_ref.shape[1]
    rows = GROUP * 8

    def place(xx, zz):
        return lax.rem(xx, NX) * NL + lax.rem(zz, NL)

    def at(dy, dz):
        return member(y + dy, zh + dz, core)

    twin = member(y, zh, 1 - core)
    z_up, z_down, y_up, y_down = at(0, 1), at(0, 3), at(1, 0), at(3, 0)
    x_up, x_down = place(x + 1, zl), place(x + 3, zl)

    reads = [pltpu.make_async_copy(src, dst, isem.at[i])
             for i, (src, dst) in enumerate(((x_hbm, x_ref), (c_hbm, c_ref),
                                             (routes_hbm, routes_ref), (rt_hbm, rt)))]
    for copy in reads:
        copy.start()
    loads = [pltpu.make_async_copy(w, wts.at[i], wsem.at[i])
             for i, w in enumerate((wg_hbm, wu_hbm, wd_hbm))]
    for copy in loads:
        copy.start()

    barrier = pltpu.get_barrier_semaphore()
    near = [at(0, 1), at(0, 2), at(0, 3), at(1, 0), at(2, 0), at(3, 0), twin]
    wide = [place(x + k, zl) for k in (1, 2, 3)] + [place(x, zl + k) for k in (1, 2, 3)]
    for peer in near:
        pl.semaphore_signal(barrier, inc=1, device_id={"expert": peer}, device_id_type=MESH)
    for peer in wide:
        pl.semaphore_signal(barrier, inc=1, device_id={"dp": peer}, device_id_type=MESH)
    for copy in reads:
        copy.wait()
    lanes = lax.broadcasted_iota(jnp.int32, m_ref.shape, 1)
    m_ref[...] = sum((routes_ref[:, k : k + 1] == lanes).astype(F32)
                     for k in range(routes_ref.shape[1]))
    pl.semaphore_wait(barrier, len(near) + len(wide))

    sent = []

    def remote(src, dst, send_sem, recv_sem, axis, target):
        return pltpu.make_async_remote_copy(
            src_ref=src, dst_ref=dst, send_sem=send_sem, recv_sem=recv_sem,
            device_id={axis: target}, device_id_type=MESH,
        )

    def go_on(*args):
        copy = remote(*args)
        copy.start()
        sent.append(copy)

    def landed(ref, sem):
        remote(ref, ref, sem, sem, "expert", twin).wait_recv()

    ins, outs = (x_ref, c_ref), (xg, cg)
    used = [0, 0]

    def send(a, dy, dz, target, own=False):
        block = lax.rem(y + dy, NY), lax.rem(zh + dz, NZ), core
        go_on(ins[a] if own else outs[a].at[block], outs[a].at[block],
              as_.at[a, used[a]], ar.at[a, member(*block)], "expert", target)
        used[a] += 1

    def arrive(a, dy, dz):
        block = lax.rem(y + dy, NY), lax.rem(zh + dz, NZ), core
        landed(outs[a].at[block], ar.at[a, member(*block)])

    def arrive_twin(a):
        for i in range(NY * NZ):
            landed(outs[a].at[i // NZ, i % NZ, 1 - core], ar.at[a, 2 * i + 1 - core])

    def spread(a, dz, own=False):
        for target in (y_up, y_down, at(2, 0), twin):
            send(a, 0, dz, target, own)

    def from_z(a, dz):
        arrive(a, 0, dz)
        spread(a, dz)

    def from_y(a, dy, dz):
        arrive(a, dy, dz)
        send(a, dy, dz, twin)

    cols = d // NX

    def lane(xx):
        return pl.ds(pl.multiple_of(lax.rem(xx, NX) * cols, cols), cols)

    def slice_out(dz):
        zz = lax.rem(zh + dz, NZ)
        for a in range(2):
            for k in (2, 1, 3):
                go_on(outs[a].at[:, zz, core, :, lane(x + k)], slices.at[a, k - 1, :, zz, core],
                      es.at[a, k - 1, dz], er.at[a, k - 1, zz], "dp", place(x + k, zl))

    def slice_twin(dz):
        zz = lax.rem(zh + dz, NZ)
        for a in range(2):
            for k in (1, 3, 2):
                ref = slices.at[a, k - 1, :, zz, core]
                landed(ref, er.at[a, k - 1, zz])
                go_on(ref, ref, ts.at[a, k - 1, dz], tr.at[a, k - 1, zz], "expert", twin)

    def slice_in(a):
        for k in (1, 3, 2):
            for zz in range(NZ):
                landed(slices.at[a, k - 1, :, zz, 1 - core], tr.at[a, k - 1, zz])

    class Small:
        def __init__(self, src, out, ssem, rsem, local):
            self.src, self.out, self.ssem, self.rsem, self.used = src, out, ssem, rsem, 0
            self.keep = pltpu.make_async_copy(src, out.at[j], local)

        def send(self, block, target, own=False):
            go_on(self.src if own else self.out.at[block], self.out.at[block],
                  self.ssem.at[self.used], self.rsem.at[block], "expert", target)
            self.used += 1

        def arrive(self, block):
            landed(self.out.at[block], self.rsem.at[block])

        def first(self):
            for k in (1, 2, 3):
                self.send(j, at(0, k), True)
            for k in (1, 2, 3):
                self.send(j, at(k, 0), True)
            self.send(j, twin, True)
            self.keep.start()

        def second(self):
            for k in (1, 3, 2):
                self.arrive(at(0, k))
                for target in (y_up, at(2, 0), y_down, twin):
                    self.send(at(0, k), target)

        def third(self):
            for dz in (0, 1, 3, 2):
                for dy in (1, 3, 2):
                    self.arrive(at(dy, dz))
                    self.send(at(dy, dz), twin)

        def last(self):
            self.keep.wait()
            for i in range(NY * NZ):
                self.arrive(2 * i + 1 - core)

    marks = Small(m_ref, mg, ms, mr, ml.at[0])
    pulls = Small(prow, pg, ps, pr, ml.at[1])

    for a in range(2):
        for k in (1, 3, 2):
            send(a, 0, 0, at(0, k), True)
        if a == 0:
            marks.first()
    for a in range(2):
        spread(a, 0, True)
    held = [pltpu.make_async_copy(ins[a], outs[a].at[y, zh, core], al.at[a]) for a in range(2)]
    for copy in held:
        copy.start()
    for a in range(2):
        for dy in (3, 1, 2):
            from_y(a, dy, 0)
    for copy in loads + held:
        copy.wait()
    slice_out(0)
    for a in range(2):
        for dz in (3, 1):
            from_z(a, dz)
    marks.second()
    for dz in (3, 1):
        for a in range(2):
            for dy in (3, 1):
                from_y(a, dy, dz)
    for a in range(2):
        from_z(a, 2)
    for dz in (3, 1):
        for a in range(2):
            from_y(a, 2, dz)
        slice_out(dz)
    marks.third()
    for a in range(2):
        for dy in (3, 1, 2):
            from_y(a, dy, 2)
    slice_out(2)
    marks.last()
    arrive_twin(0)

    xv, cv = xg.reshape(rows, d), cg.reshape(rows, d)
    mask = jnp.transpose(mg.reshape(rows, 128)[...])[:8]
    logits = regroup(dot(thirds(rt[...]), xv[...], ((1,), (1,))))
    affinity = jax.nn.sigmoid(logits)
    denominator = jnp.sum(affinity * mask, axis=0, keepdims=True)
    gates = mask * affinity / denominator
    wide_gates = jnp.transpose(jnp.concatenate([gates, jnp.zeros((120, rows), F32)], axis=0))
    mine = lax.broadcasted_iota(jnp.int32, wide_gates.shape, 1) == lax.div(j, 4)
    gate = jnp.sum(jnp.where(mine, wide_gates, 0.0), axis=1, keepdims=True)
    gate_pre[...] = dot(xv[...], wts[0], ((1,), (0,)))
    up_pre[...] = dot(xv[...], wts[1], ((1,), (0,)))
    arrive_twin(1)
    pull[...] = dot(cv[...], wts[2], ((1,), (0,)))
    sigma = jax.nn.sigmoid(gate_pre[...])
    silu = gate_pre[...] * sigma
    hidden = silu * up_pre[...]
    hs, dg, du = acts.at[0, 0], acts.at[0, 1], acts.at[0, 2]
    hs[...] = (gate * hidden).astype(BF16)
    prow[...] = jnp.sum(jnp.transpose(hidden * pull[...]), axis=0, keepdims=True)
    hidden_grad = gate * pull[...]
    dg[...] = (hidden_grad * up_pre[...] * sigma
               * (1.0 + gate_pre[...] * (1.0 - sigma))).astype(BF16)
    du[...] = (hidden_grad * silu).astype(BF16)

    half = rows // 2
    ends = pl.ds(0, half), pl.ds(half, half)

    def acts_first(p):
        go_on(acts.at[0, p], acts.at[1, p], xs.at[p, 0], xr.at[p, 0], "dp", x_up)
        go_on(acts.at[0, p], acts.at[3, p], xs.at[p, 1], xr.at[p, 1], "dp", x_down)

    def acts_second(p):
        for h in range(2):
            landed(acts.at[(1, 3)[h], p], xr.at[p, h])
            go_on(acts.at[(1, 3)[h], p, ends[h]], acts.at[2, p, ends[h]], vs.at[p, h],
                  vr.at[p, h], "dp", (x_up, x_down)[h])

    def weight_rows(p):
        for h in range(2):
            landed(acts.at[2, p, ends[h]], vr.at[p, h])
        a = 0 if p else 1
        value = dot((cv, xv)[p > 0][:, lane(x)], acts[0, p], ((0,), (0,)))
        for k in (1, 2, 3):
            other = slices.at[a, k - 1].reshape(rows, cols)
            value = value + dot(other[...], acts[k, p], ((0,), (0,)))
        dw[p] = value.astype(BF16).reshape(dw.shape[1:])

    writes = []

    def write(src, dst, i):
        copy = pltpu.make_async_copy(src, dst, osem.at[i])
        copy.start()
        writes.append(copy)

    is_end = jnp.logical_or(zl == 0, zl == NL - 1)

    def hop(p, k, to_aid):
        shard = dw.at[p, lax.rem(zl + k, NL)]
        if to_aid:
            return remote(shard, aid.at[p], hs_.at[p], hr.at[p], "dp", place(x, zl + NL - k))
        return remote(shard, zo.at[p, k], us.at[p, k - 1], ur.at[p, k - 1], "dp",
                      place(x, zl + k))

    def across_first(p):
        for k, end in ((3, 0), (1, NL - 1)):
            @pl.when(zl == end)
            def _():
                hop(p, k, True).start()

            @pl.when(zl != end)
            def _():
                hop(p, k, False).start()

        @pl.when(is_end)
        def _():
            hop(p, 2, False).start()

        zo[p, 0] = dw[p, zl]

        @pl.when(zl == 0)
        def _():
            zo[p, 1] = jnp.zeros(zo.shape[2:], BF16)

        @pl.when(zl == NL - 1)
        def _():
            zo[p, 3] = jnp.zeros(zo.shape[2:], BF16)

    def across_second(p):
        @pl.when(jnp.logical_not(is_end))
        def _():
            landed(aid.at[p], hr.at[p])
            aid[p] = (dw[p, lax.rem(zl + 2, NL)].astype(F32) + aid[p].astype(F32)).astype(BF16)
            remote(aid.at[p], zo.at[p, 2], us.at[p, 1], ur.at[p, 1], "dp",
                   place(x, zl + 2)).start()

    def across_last(p):
        landed(zo.at[p, 2], ur.at[p, 1])
        hop(p, 2, False).wait_send()
        for k, end, none in ((3, 0, NL - 1), (1, NL - 1, 0)):
            @pl.when(zl == end)
            def _():
                hop(p, k, True).wait_send()

            @pl.when(zl != end)
            def _():
                hop(p, k, False).wait_send()

            @pl.when(zl != none)
            def _():
                landed(zo.at[p, k], ur.at[p, k - 1])

        wo[p] = (zo[p, 0].astype(F32) + zo[p, 1].astype(F32)
                 + zo[p, 2].astype(F32) + zo[p, 3].astype(F32))
        write(wo.at[p], wo_hbm.at[p], p)

    def start_core(a):
        for dy in (2, 1, 3, 0):
            yy = lax.rem(y + dy, NY)
            go_on(part.at[a, yy, :, 1 - core], cbuf.at[a, yy], cs.at[a, dy], cr.at[a, yy],
                  "expert", twin)

    def add_core(a, dy):
        yy = lax.rem(y + dy, NY)
        landed(cbuf.at[a, yy], cr.at[a, yy])

        @pl.loop(0, NZ)
        def _(k):
            q[a, yy, k] = (part[a, yy, k, core].astype(F32)
                           + cbuf[a, yy, k].astype(F32)).astype(BF16)

    y1, y2, y3 = lax.rem(y + 1, NY), lax.rem(y + 2, NY), lax.rem(y + 3, NY)

    def row(k):
        return lax.rem(zh + k, NZ)

    def y_start(k):
        zz = row(k)
        for a in range(2):
            go_on(q.at[a, y2, zz], s1.at[a, zz], ys.at[a, 0, k], yr.at[a, 0, k], "expert",
                  (y_up, y_down)[a])

    def y_plain(k):
        zz = row(k)
        go_on(q.at[1, y1, zz], fy.at[1, 0, zz], ys.at[1, 1, k], yr.at[1, 1, k], "expert", y_up)
        go_on(q.at[0, y3, zz], fy.at[0, 1, zz], ys.at[0, 2, k], yr.at[0, 2, k], "expert", y_down)

    def y_first():
        for dy in (2, 1, 3):
            for a in range(2):
                add_core(a, dy)
        y_start(2)
        y_plain(2)
        y_start(1)
        for a in range(2):
            add_core(a, 0)

    def y_pass(k):
        zz = row(k)
        for a in range(2):
            landed(s1.at[a, zz], yr.at[a, 0, k])
            s1[a, zz] = (q[a, (y1, y3)[a], zz].astype(F32) + s1[a, zz].astype(F32)).astype(BF16)
            go_on(s1.at[a, zz], fy.at[a, a, zz], ys.at[a, 1 + a, k], yr.at[a, 1 + a, k], "expert",
                  (y_up, y_down)[a])

    h1, h2, h3 = lax.rem(zh + 1, NZ), lax.rem(zh + 2, NZ), lax.rem(zh + 3, NZ)

    def y_end(k):
        zz = row(k)
        for a in range(2):
            for s in range(2):
                landed(fy.at[a, s, zz], yr.at[a, 1 + s, k])
            r[a, zz] = (q[a, y, zz].astype(F32) + fy[a, 0, zz].astype(F32)
                        + fy[a, 1, zz].astype(F32)).astype(BF16)
            if k == 2:
                go_on(r.at[a, zz], s1z.at[a], zs.at[a, 0], zr.at[a, 0], "expert",
                      (z_up, z_down)[a])
        if k == 1:
            go_on(r.at[1, zz], fz.at[1, 0], zs.at[1, 1], zr.at[1, 1], "expert", z_up)
        if k == 3:
            go_on(r.at[0, zz], fz.at[0, 1], zs.at[0, 2], zr.at[0, 2], "expert", z_down)

    def z_second():
        for a in range(2):
            landed(s1z.at[a], zr.at[a, 0])
            r2[a] = (r[a, (h1, h3)[a]].astype(F32) + s1z[a].astype(F32)).astype(BF16)
            go_on(r2.at[a], fz.at[a, a], zs.at[a, 1 + a], zr.at[a, 1 + a], "expert",
                  (z_up, z_down)[a])

    def z_third(a):
        for s in range(2):
            landed(fz.at[a, s], zr.at[a, 1 + s])
        return r[a, zh].astype(F32) + fz[a, 0].astype(F32) + fz[a, 1].astype(F32)

    def router_first():
        sums = []
        for e in range(8):
            sums.append(pg[4 * e] + pg[4 * e + 1] + pg[4 * e + 2] + pg[4 * e + 3])
        full = jnp.concatenate(sums, axis=0)
        mean = jnp.sum(gates * full, axis=0, keepdims=True)
        lt[...] = mask * (full - mean) / denominator * affinity * (1.0 - affinity)
        value = regroup(dot(thirds(lt[...]), xv[...], ((1,), (0,))))
        for k in range(NX):
            gx[k] = value[:, k * cols : (k + 1) * cols]
        for k in (1, 2, 3):
            go_on(gx.at[lax.rem(x + k, NX)], gx.at[NX + k - 1], gs.at[0, k - 1],
                  gr.at[0, k - 1], "dp", place(x + k, zl))

    def router_second():
        for k in range(3):
            landed(gx.at[NX + k], gr.at[0, k])
        gsum[...] = gx[x] + gx[NX] + gx[NX + 1] + gx[NX + 2]
        for k in (1, 2, 3):
            go_on(gsum, go.at[zl, :, lane(x)], gs.at[1, k - 1], gr.at[1, k - 1], "dp",
                  place(x, zl + k))
        keep = pltpu.make_async_copy(gsum, go.at[zl, :, lane(x)], gl)
        keep.start()
        keep.wait()

    def router_third():
        for k in (1, 2, 3):
            landed(go.at[lax.rem(zl + NL - k, NL), :, lane(x)], gr.at[1, k - 1])
        for k in (1, 2, 3):
            go_on(go.at[:, :, lane(x)], go.at[:, :, lane(x)], gs.at[2, k - 1], gr.at[2, k - 1],
                  "dp", place(x + k, zl))

    def router_last():
        for k in (1, 2, 3):
            landed(go.at[:, :, lane(x + NX - k)], gr.at[2, k - 1])

    acts_first(0)
    acts_first(1)
    pulls.first()
    part.reshape(2, rows, d)[0] = dot(hs[...], wts[2], ((1,), (1,))).astype(BF16)
    start_core(0)
    part.reshape(2, rows, d)[1] = (dot(dg[...], wts[0], ((1,), (1,)))
                                   + dot(du[...], wts[1], ((1,), (1,)))).astype(BF16)
    start_core(1)
    y_first()
    for dz in (0, 3, 1):
        slice_twin(dz)
    y_pass(2)
    y_plain(1)
    y_start(3)
    acts_second(0)
    acts_first(2)
    y_pass(1)
    y_plain(3)
    y_start(0)
    y_end(2)
    slice_twin(2)
    y_pass(3)
    y_plain(0)
    y_end(1)
    slice_in(1)
    weight_rows(0)
    across_first(0)
    acts_second(1)
    y_pass(0)
    y_end(3)
    pulls.second()
    acts_second(2)
    y_end(0)
    slice_in(0)
    weight_rows(1)
    pulls.third()
    z_second()
    across_first(1)
    pulls.last()
    router_first()
    weight_rows(2)
    router_second()
    across_first(2)
    across_second(0)
    across_second(1)
    across_second(2)
    router_third()
    to[0] = z_third(0)
    total = z_third(1)
    ours = lax.broadcasted_iota(jnp.int32, (8, rows), 0) + 8 * j
    pick = lax.broadcasted_iota(jnp.int32, (8, rows), 1) == ours
    for e in range(8):
        weight = jnp.sum(jnp.where(pick, lt[e : e + 1, :], 0.0), axis=1, keepdims=True)
        total = total + weight * rt[e : e + 1, :]
    to[1] = total
    write(to, to_hbm, 3)
    router_last()
    gout[...] = go[0] + go[1] + go[2] + go[3]
    write(gout, go_hbm, 4)
    for p in range(3):
        across_last(p)
    for copy in sent:
        copy.wait_send()
    for copy in writes:
        copy.wait()


def layer(tokens, cotangent, routes, router_t, w_gate, w_up, w_down):
    d = tokens.shape[1]
    f = w_gate.shape[1]
    rows = GROUP * 8
    n = d // (NX * NL)
    cols = d // NX
    dma = pltpu.SemaphoreType.DMA
    return pl.pallas_call(
        layer_kernel,
        out_shape=[
            jax.ShapeDtypeStruct((3, n, f), F32),
            jax.ShapeDtypeStruct((2, 8, d), F32),
            jax.ShapeDtypeStruct((8, d), F32),
        ],
        in_specs=[ANY] * 7,
        out_specs=[ANY] * 3,
        scratch_shapes=[
            pltpu.VMEM((8, d), BF16),
            pltpu.VMEM((8, d), BF16),
            pltpu.VMEM(routes.shape, jnp.int32),
            pltpu.VMEM(router_t.shape, F32),
            pltpu.VMEM((3, NL, n, f), BF16),
            pltpu.VMEM((NL, 8, d), F32),
            pltpu.VMEM((3, n, f), F32),
            pltpu.VMEM((2, 8, d), F32),
            pltpu.VMEM((8, d), F32),
            pltpu.VMEM((NY, NZ, 2, 8, d), BF16),
            pltpu.VMEM((NY, NZ, 2, 8, d), BF16),
            pltpu.VMEM((GROUP, 8, 128), F32),
            pltpu.VMEM((8, 128), F32),
            pltpu.VMEM((GROUP, 1, rows), F32),
            pltpu.VMEM((1, rows), F32),
            pltpu.VMEM((3, d, f), BF16),
            pltpu.VMEM((rows, f), F32),
            pltpu.VMEM((rows, f), F32),
            pltpu.VMEM((rows, f), F32),
            pltpu.VMEM((NX, 3, rows, f), BF16),
            pltpu.VMEM((8, rows), F32),
            pltpu.VMEM((2, NY, NZ, 2, 8, d), BF16),
            pltpu.VMEM((2, NY, NZ, 8, d), BF16),
            pltpu.VMEM((2, NY, NZ, 8, d), BF16),
            pltpu.VMEM((2, NZ, 8, d), BF16),
            pltpu.VMEM((2, 2, NZ, 8, d), BF16),
            pltpu.VMEM((2, NZ, 8, d), BF16),
            pltpu.VMEM((2, 8, d), BF16),
            pltpu.VMEM((2, 2, 8, d), BF16),
            pltpu.VMEM((2, 8, d), BF16),
            pltpu.VMEM((3, NL, n, f), BF16),
            pltpu.VMEM((2, NX - 1, NY, NZ, 2, 8, cols), BF16),
            pltpu.VMEM((3, n, f), BF16),
            pltpu.VMEM((NX + 3, 8, cols), F32),
            pltpu.VMEM((8, cols), F32),
            dma((4,)), dma((5,)), dma((3,)), dma((2, 31)), dma((2, GROUP)), dma((2,)),
            dma((31,)), dma((GROUP,)), dma((31,)), dma((GROUP,)), dma((2,)),
            dma((2, NY)), dma((2, NY)), dma((2, 3, NZ)), dma((2, 3, NZ)), dma((2, 3)), dma((2, 3)),
            dma((2, 3, NZ)), dma((2, 3, NZ)), dma((2, 3, NZ)), dma((2, 3, NZ)),
            dma((3, 2)), dma((3, 2)), dma((3, 2)), dma((3, 2)),
            dma((3, 3)), dma((3, 3)), dma((3,)), dma((3,)), dma((3, 3)), dma((3, 3)), dma,
        ],
        compiler_params=pltpu.CompilerParams(collective_id=0, has_side_effects=True),
        name="moe_layer",
    )(tokens, cotangent, routes, router_t, w_gate, w_up, w_down)


def finish_kernel(w, t, g, mo, to, go, o0, o1, o2):
    mo[...] = t[0].astype(BF16)
    to[...] = t[1].astype(BF16)
    go[...] = g[...]
    o0[...] = w[1]
    o1[...] = w[2]
    o2[...] = w[0]


def finish(w, t, g):
    grad = jax.ShapeDtypeStruct(w.shape[1:], F32)
    token = jax.ShapeDtypeStruct(t.shape[1:], BF16)
    return pl.pallas_call(
        finish_kernel,
        out_shape=[token, token, jax.ShapeDtypeStruct(g.shape, F32), grad, grad, grad],
        in_specs=[VMEM] * 3,
        out_specs=[VMEM] * 6,
        name="finish",
    )(w, t, g)


def local(tokens, routes, router, w_gate, w_up, w_down, cotangent):
    parts = layer(tokens, cotangent, routes, router.T, w_gate, w_up, w_down)
    mixed, grad_tokens, grad_router, grad_gate, grad_up, grad_down = finish(*parts)
    return (mixed, grad_tokens, grad_router.T, grad_gate, grad_up, grad_down)


def solution(mesh):
    return jax.shard_map(
        local,
        mesh=mesh,
        in_specs=(
            P(("dp", "expert"), None),
            P(("dp", "expert"), None),
            P(),
            P(None, "expert"),
            P(None, "expert"),
            P(None, "expert"),
            P(("dp", "expert"), None),
        ),
        out_specs=(
            P(("dp", "expert"), None),
            P(("dp", "expert"), None),
            P(),
            P("dp", "expert"),
            P("dp", "expert"),
            P("dp", "expert"),
        ),
        check_vma=False,
    )
```

```python
import jax
import jax.numpy as jnp
from jax import lax
from jax.experimental import pallas as pl
from jax.experimental.pallas import tpu as pltpu
from jax.sharding import PartitionSpec as P

NY = 4
NZ = 4
NX = 4
NL = 4
GROUP = 2 * NY * NZ
MESH = pl.DeviceIdType.MESH
VMEM = pl.BlockSpec(memory_space=pltpu.VMEM)
ANY = pl.BlockSpec(memory_space=pl.ANY)
F32 = jnp.float32
BF16 = jnp.bfloat16


def member(y, zh, core):
    return (lax.rem(y, NY) * NZ + lax.rem(zh, NZ)) * 2 + core


def dot(a, b, contract):
    return lax.dot_general(a, b, (contract, ((), ())), preferred_element_type=F32)


def thirds(a):
    one = a.astype(BF16).astype(F32)
    two = (a - one).astype(BF16).astype(F32)
    return jnp.concatenate([one, two, a - one - two], axis=0).astype(BF16)


def regroup(a):
    n = a.shape[0] // 3
    return a[:n] + a[n : 2 * n] + a[2 * n :]


def layer_kernel(x_hbm, c_hbm, routes_hbm, rt_hbm, wg_hbm, wu_hbm, wd_hbm,
                 wo_hbm, to_hbm, go_hbm,
                 x_ref, c_ref, routes_ref, rt, zo, gz, wo, to, gout,
                 xg, cg, mg, m_ref, pg, prow, wts, gate_pre, up_pre, pull, acts, lt,
                 part, cbuf, q, s1, fy, r, s1z, fz, r2,
                 dw, slices, aid, gx, gsum, gtot,
                 isem, osem, wsem, as_, ar, al, ms, mr, ps, pr, ml, cs, cr, ys, yr, zs, zr,
                 es, er, ts, tr, xs, xr, vr, us, ur, hr, gs, gr):
    j = lax.axis_index("expert")
    core = lax.rem(j, 2)
    zh = lax.rem(lax.div(j, 2), NZ)
    y = lax.div(j, 2 * NZ)
    dev = lax.axis_index("dp")
    x, zl = lax.div(dev, NL), lax.rem(dev, NL)
    d = x_ref.shape[1]
    rows = GROUP * 8

    def place(xx, zz):
        return lax.rem(xx, NX) * NL + lax.rem(zz, NL)

    def at(dy, dz):
        return member(y + dy, zh + dz, core)

    twin = member(y, zh, 1 - core)
    z_up, z_down, y_up, y_down = at(0, 1), at(0, 3), at(1, 0), at(3, 0)
    x_up, x_down = place(x + 1, zl), place(x + 3, zl)

    reads = [pltpu.make_async_copy(src, dst, isem.at[i])
             for i, (src, dst) in enumerate(((x_hbm, x_ref), (c_hbm, c_ref),
                                             (routes_hbm, routes_ref), (rt_hbm, rt)))]
    for copy in reads:
        copy.start()
    loads = [pltpu.make_async_copy(w, wts.at[i], wsem.at[i])
             for i, w in enumerate((wg_hbm, wu_hbm, wd_hbm))]
    for copy in loads:
        copy.start()

    barrier = pltpu.get_barrier_semaphore()
    near = [at(0, 1), at(0, 2), at(0, 3), at(1, 0), at(2, 0), at(3, 0), twin]
    wide = [place(x + k, zl) for k in (1, 2, 3)] + [place(x, zl + k) for k in (1, 2, 3)]
    for peer in near:
        pl.semaphore_signal(barrier, inc=1, device_id={"expert": peer}, device_id_type=MESH)
    for peer in wide:
        pl.semaphore_signal(barrier, inc=1, device_id={"dp": peer}, device_id_type=MESH)
    for copy in reads:
        copy.wait()
    lanes = lax.broadcasted_iota(jnp.int32, m_ref.shape, 1)
    m_ref[...] = sum((routes_ref[:, k : k + 1] == lanes).astype(F32)
                     for k in range(routes_ref.shape[1]))
    pl.semaphore_wait(barrier, len(near) + len(wide))


    def remote(src, dst, send_sem, recv_sem, axis, target):
        return pltpu.make_async_remote_copy(
            src_ref=src, dst_ref=dst, send_sem=send_sem, recv_sem=recv_sem,
            device_id={axis: target}, device_id_type=MESH,
        )

    def go_on(*args):
        remote(*args).start()

    def landed(ref, sem):
        remote(ref, ref, sem, sem, "expert", twin).wait_recv()

    def gone(ref, sem):
        remote(ref, ref, sem, sem, "expert", twin).wait_send()

    ins, outs = (x_ref, c_ref), (xg, cg)
    three = cbuf.at[0, 0, pl.ds(0, 3)]

    def send(a, dy, dz, target, sem, own=False):
        block = lax.rem(y + dy, NY), lax.rem(zh + dz, NZ), core
        go_on(ins[a] if own else outs[a].at[block], outs[a].at[block],
              as_.at[a], ar.at[a, sem], "expert", target)

    def arrive_twin(a):
        landed(outs[a].at[:, :, 1 - core], ar.at[a, 7])

    def spread(a, dz, own=False):
        for target in (y_up, y_down, at(2, 0)):
            send(a, 0, dz, target, 3 + dz, own)
        send(a, 0, dz, twin, 7, own)

    def from_z(a, dz):
        landed(outs[a].at[y, lax.rem(zh + dz, NZ), core], ar.at[a, dz - 1])
        spread(a, dz)

    def from_y(a, dz):
        landed(three, ar.at[a, 3 + dz])
        for dy in (3, 1, 2):
            send(a, dy, dz, twin, 7)

    cols = d // NX

    def lane(xx):
        return pl.ds(pl.multiple_of(lax.rem(xx, NX) * cols, cols), cols)

    def slice_out(a, dz):
        zz = lax.rem(zh + dz, NZ)
        for k in (2, 1, 3):
            go_on(outs[a].at[:, zz, core, :, lane(x + k)], slices.at[a, k - 1, :, zz, core],
                  es, er.at[a], "dp", place(x + k, zl))

    def slice_twin(a):
        ref = slices.at[a, :, :, :, core]
        landed(ref, er.at[a])
        go_on(ref, ref, ts, tr.at[a], "expert", twin)

    def slice_in(a):
        landed(slices.at[a, :, :, :, 1 - core], tr.at[a])

    class Small:
        def __init__(self, src, out, ssem, rsem, local):
            self.src, self.out, self.ssem, self.rsem = src, out, ssem, rsem
            self.keep = pltpu.make_async_copy(src, out.at[j], local)

        def send(self, block, target, sem, own=False):
            go_on(self.src if own else self.out.at[block], self.out.at[block],
                  self.ssem, self.rsem.at[sem], "expert", target)

        def spread(self, dz, own=False):
            for target in (y_up, y_down, at(2, 0)):
                self.send(at(0, dz), target, 3 + dz, own)
            self.send(at(0, dz), twin, 7, own)

        def first(self):
            for k in (1, 2, 3):
                self.send(j, at(0, k), 3 - k, True)
            self.spread(0, True)
            self.keep.start()

        def second(self):
            for dz in (1, 3, 2):
                landed(self.out.at[at(0, dz)], self.rsem.at[dz - 1])
                self.spread(dz)

        def third(self):
            for dz in (0, 1, 3, 2):
                landed(self.out.at[pl.ds(0, 3)], self.rsem.at[3 + dz])
                for dy in (1, 3, 2):
                    self.send(at(dy, dz), twin, 7)

        def last(self):
            self.keep.wait()
            landed(self.out.at[pl.ds(0, NY * NZ)], self.rsem.at[7])

        def done(self):
            gone(self.out.at[pl.ds(0, GROUP - 1)], self.ssem)

    marks = Small(m_ref, mg, ms, mr, ml.at[0])
    pulls = Small(prow, pg, ps, pr, ml.at[1])

    for a in range(2):
        for k in (1, 3, 2):
            send(a, 0, 0, at(0, k), 3 - k, True)
        if a == 0:
            marks.first()
    for a in range(2):
        spread(a, 0, True)
    held = [pltpu.make_async_copy(ins[a], outs[a].at[y, zh, core], al.at[a]) for a in range(2)]
    for copy in held:
        copy.start()
    def all_y(a, dz):
        from_y(a, dz)
        slice_out(a, dz)

    for copy in loads + held:
        copy.wait()
    all_y(0, 0)
    for dz in (3, 1, 2):
        from_z(0, dz)
    marks.second()
    all_y(1, 0)
    for dz in (3, 1):
        from_z(1, dz)
    for dz in (3, 1, 2):
        all_y(0, dz)
    marks.third()
    from_z(1, 2)
    arrive_twin(0)

    xv, cv = xg.reshape(rows, d), cg.reshape(rows, d)
    gate_pre[...] = dot(xv[...], wts[0], ((1,), (0,)))
    up_pre[...] = dot(xv[...], wts[1], ((1,), (0,)))
    logits = regroup(dot(thirds(rt[...]), xv[...], ((1,), (1,))))
    affinity = jax.nn.sigmoid(logits)
    for dz in (3, 1):
        all_y(1, dz)
    marks.last()
    mask = jnp.transpose(mg.reshape(rows, 128)[...])[:8]
    denominator = jnp.sum(affinity * mask, axis=0, keepdims=True)
    gates = mask * affinity / denominator
    wide_gates = jnp.transpose(jnp.concatenate([gates, jnp.zeros((120, rows), F32)], axis=0))
    mine = lax.broadcasted_iota(jnp.int32, wide_gates.shape, 1) == lax.div(j, 4)
    gate = jnp.sum(jnp.where(mine, wide_gates, 0.0), axis=1, keepdims=True)
    hs, dg, du = acts.at[0, 0], acts.at[0, 1], acts.at[0, 2]
    hs[...] = (gate * (gate_pre[...] * jax.nn.sigmoid(gate_pre[...]) * up_pre[...])).astype(BF16)

    def hidden_back():
        pull[...] = dot(cv[...], wts[2], ((1,), (0,)))
        sigma = jax.nn.sigmoid(gate_pre[...])
        silu = gate_pre[...] * sigma
        hidden = silu * up_pre[...]
        prow[...] = jnp.sum(jnp.transpose(hidden * pull[...]), axis=0, keepdims=True)
        hidden_grad = gate * pull[...]
        dg[...] = (hidden_grad * up_pre[...] * sigma
                   * (1.0 + gate_pre[...] * (1.0 - sigma))).astype(BF16)
        du[...] = (hidden_grad * silu).astype(BF16)

    half = rows // 2
    ends = pl.ds(0, half), pl.ds(half, half)

    def acts_first(p):
        go_on(acts.at[0, p], acts.at[1, p], xs, xr.at[p, 0], "dp", x_up)
        go_on(acts.at[0, p], acts.at[3, p], xs, xr.at[p, 1], "dp", x_down)

    def acts_second(p):
        for h in range(2):
            landed(acts.at[(1, 3)[h], p], xr.at[p, h])
            go_on(acts.at[(1, 3)[h], p, ends[h]], acts.at[2, p, ends[h]], xs,
                  vr.at[p], "dp", (x_up, x_down)[h])

    def weight_rows(p):
        landed(acts.at[2, p], vr.at[p])
        a = 0 if p else 1
        value = dot((cv, xv)[p > 0][:, lane(x)], acts[0, p], ((0,), (0,)))
        for k in (1, 2, 3):
            other = slices.at[a, k - 1].reshape(rows, cols)
            value = value + dot(other[...], acts[k, p], ((0,), (0,)))
        dw[p] = value.astype(BF16).reshape(dw.shape[1:])

    writes = []

    def write(src, dst, i):
        copy = pltpu.make_async_copy(src, dst, osem.at[i])
        copy.start()
        writes.append(copy)

    is_end = jnp.logical_or(zl == 0, zl == NL - 1)

    def hop(p, k, to_aid):
        shard = dw.at[p, lax.rem(zl + k, NL)]
        if to_aid:
            return remote(shard, aid.at[p], us, hr.at[p], "dp", place(x, zl + NL - k))
        return remote(shard, zo.at[p, k], us, ur.at[p, k - 1], "dp",
                      place(x, zl + k))

    def across_first(p):
        for k, end in ((3, 0), (1, NL - 1)):
            @pl.when(zl == end)
            def _():
                hop(p, k, True).start()

            @pl.when(zl != end)
            def _():
                hop(p, k, False).start()

        @pl.when(is_end)
        def _():
            hop(p, 2, False).start()

        zo[p, 0] = dw[p, zl]

        @pl.when(zl == 0)
        def _():
            zo[p, 1] = jnp.zeros(zo.shape[2:], BF16)

        @pl.when(zl == NL - 1)
        def _():
            zo[p, 3] = jnp.zeros(zo.shape[2:], BF16)

    def across_second(p):
        @pl.when(jnp.logical_not(is_end))
        def _():
            landed(aid.at[p], hr.at[p])
            aid[p] = (dw[p, lax.rem(zl + 2, NL)].astype(F32) + aid[p].astype(F32)).astype(BF16)
            remote(aid.at[p], zo.at[p, 2], us, ur.at[p, 1], "dp",
                   place(x, zl + 2)).start()

    def across_last(p):
        landed(zo.at[p, 2], ur.at[p, 1])
        for k, none in ((3, NL - 1), (1, 0)):
            @pl.when(zl != none)
            def _():
                landed(zo.at[p, k], ur.at[p, k - 1])

        wo[p] = (zo[p, 0].astype(F32) + zo[p, 1].astype(F32)
                 + zo[p, 2].astype(F32) + zo[p, 3].astype(F32))
        write(wo.at[p], wo_hbm.at[p], p)

    def start_core(a):
        for dy in (2, 1, 3, 0):
            yy = lax.rem(y + dy, NY)
            go_on(part.at[a, yy, :, 1 - core], cbuf.at[a, yy], cs, cr.at[a, yy],
                  "expert", twin)

    def add_core(a, dy):
        yy = lax.rem(y + dy, NY)
        landed(cbuf.at[a, yy], cr.at[a, yy])

        @pl.loop(0, NZ)
        def _(k):
            q[a, yy, k] = (part[a, yy, k, core].astype(F32)
                           + cbuf[a, yy, k].astype(F32)).astype(BF16)

    y1, y2, y3 = lax.rem(y + 1, NY), lax.rem(y + 2, NY), lax.rem(y + 3, NY)

    def row(k):
        return lax.rem(zh + k, NZ)

    def y_start(a, k):
        zz = row(k)
        go_on(q.at[a, y2, zz], s1.at[a, zz], ys, yr.at[a, 0, k], "expert",
              (y_up, y_down)[a])

    def y_first(a):
        for dy in (2, 1, 3):
            add_core(a, dy)
        y_start(a, 2)
        y_start(a, 1)
        for k in (2, 1, 3, 0):
            go_on(q.at[a, (y3, y1)[a], row(k)], fy.at[a, 1 - a, row(k)], ys,
                  yr.at[a, 1, k], "expert", (y_down, y_up)[a])
        add_core(a, 0)

    def y_pass(a, k):
        zz = row(k)
        landed(s1.at[a, zz], yr.at[a, 0, k])
        s1[a, zz] = (q[a, (y1, y3)[a], zz].astype(F32) + s1[a, zz].astype(F32)).astype(BF16)
        go_on(s1.at[a, zz], fy.at[a, a, zz], ys, yr.at[a, 1, k], "expert",
              (y_up, y_down)[a])

    h1, h2, h3 = lax.rem(zh + 1, NZ), lax.rem(zh + 2, NZ), lax.rem(zh + 3, NZ)

    def y_end(a, k):
        zz = row(k)
        landed(fy.at[a, :, zz], yr.at[a, 1, k])
        r[a, zz] = (q[a, y, zz].astype(F32) + fy[a, 0, zz].astype(F32)
                    + fy[a, 1, zz].astype(F32)).astype(BF16)
        if k == 2:
            go_on(r.at[a, zz], s1z.at[a], zs, zr.at[a, 0], "expert", (z_up, z_down)[a])
        if k == (3, 1)[a]:
            go_on(r.at[a, zz], fz.at[a, 1 - a], zs, zr.at[a, 1], "expert",
                  (z_down, z_up)[a])

    def z_second(a):
        landed(s1z.at[a], zr.at[a, 0])
        r2[a] = (r[a, (h1, h3)[a]].astype(F32) + s1z[a].astype(F32)).astype(BF16)
        go_on(r2.at[a], fz.at[a, a], zs, zr.at[a, 1], "expert",
              (z_up, z_down)[a])

    def z_third(a):
        landed(fz.at[a], zr.at[a, 1])
        return r[a, zh].astype(F32) + fz[a, 0].astype(F32) + fz[a, 1].astype(F32)

    def router_first():
        sums = []
        for e in range(8):
            sums.append(pg[4 * e] + pg[4 * e + 1] + pg[4 * e + 2] + pg[4 * e + 3])
        full = jnp.concatenate(sums, axis=0)
        mean = jnp.sum(gates * full, axis=0, keepdims=True)
        lt[...] = mask * (full - mean) / denominator * affinity * (1.0 - affinity)
        value = regroup(dot(thirds(lt[...]), xv[...], ((1,), (0,))))
        for k in range(NX):
            gx[k] = value[:, k * cols : (k + 1) * cols]
        for k in (1, 2, 3):
            go_on(gx.at[lax.rem(x + k, NX)], gx.at[NX + k - 1], gs.at[0],
                  gr.at[0], "dp", place(x + k, zl))

    def router_second():
        landed(gx.at[pl.ds(NX, 3)], gr.at[0])
        gsum[...] = gx[x] + gx[NX] + gx[NX + 1] + gx[NX + 2]
        for k in (1, 2, 3):
            go_on(gsum, gz.at[k - 1], gs.at[1], gr.at[1], "dp", place(x, zl + k))

    def router_third():
        landed(gz, gr.at[1])
        gtot[...] = gsum[...] + gz[0] + gz[1] + gz[2]
        for k in (1, 2, 3):
            go_on(gtot, gout.at[:, lane(x)], gs.at[2], gr.at[2], "dp",
                  place(x + k, zl))
        gout[:, lane(x)] = gtot[...]

    def router_last():
        landed(gz, gr.at[2])

    acts_first(0)
    part.reshape(2, rows, d)[0] = dot(hs[...], wts[2], ((1,), (1,))).astype(BF16)
    start_core(0)
    all_y(1, 2)
    y_first(0)
    y_pass(0, 2)
    y_start(0, 3)
    acts_second(0)
    y_pass(0, 1)
    y_start(0, 0)
    arrive_twin(1)
    hidden_back()
    acts_first(1)
    acts_first(2)
    pulls.first()
    y_pass(0, 3)
    y_end(0, 2)
    part.reshape(2, rows, d)[1] = (dot(dg[...], wts[0], ((1,), (1,)))
                                   + dot(du[...], wts[1], ((1,), (1,)))).astype(BF16)
    start_core(1)
    y_pass(0, 0)
    y_end(0, 1)
    y_first(1)
    slice_twin(1)
    y_end(0, 3)
    slice_in(1)
    weight_rows(0)
    across_first(0)
    y_pass(1, 2)
    y_start(1, 3)
    y_end(0, 0)
    slice_twin(0)
    acts_second(1)
    y_pass(1, 1)
    y_start(1, 0)
    z_second(0)
    y_end(1, 2)
    y_pass(1, 3)
    acts_second(2)
    pulls.second()
    y_pass(1, 0)
    y_end(1, 1)
    slice_in(0)
    weight_rows(1)
    across_first(1)
    y_end(1, 3)
    pulls.third()
    across_second(0)
    weight_rows(2)
    across_first(2)
    pulls.last()
    router_first()
    y_end(1, 0)
    z_second(1)
    router_second()
    across_second(1)
    across_second(2)
    router_third()
    to[0] = z_third(0)
    total = z_third(1)
    ours = lax.broadcasted_iota(jnp.int32, (8, rows), 0) + 8 * j
    pick = lax.broadcasted_iota(jnp.int32, (8, rows), 1) == ours
    for e in range(8):
        weight = jnp.sum(jnp.where(pick, lt[e : e + 1, :], 0.0), axis=1, keepdims=True)
        total = total + weight * rt[e : e + 1, :]
    to[1] = total
    write(to, to_hbm, 3)
    router_last()
    write(gout, go_hbm, 4)
    for p in range(3):
        across_last(p)
    for a in range(2):
        gone(outs[a].reshape(GROUP, 8, d).at[pl.ds(0, GROUP - 1)], as_.at[a])
    marks.done()
    pulls.done()
    gone(slices.at[:, :, :, :, 0], es)
    gone(slices.at[:, :, :, :, 0], ts)
    gone(cbuf, cs)
    gone(cbuf.at[:, pl.ds(0, 3)], ys)
    gone(cbuf.at[:, 0, pl.ds(0, 3)], zs)
    gone(acts.at[pl.ds(0, 3)], xs)
    gone(zo.at[:, pl.ds(0, 3)], us)
    for i in range(3):
        gone(gz, gs.at[i])
    for copy in writes:
        copy.wait()


def layer(tokens, cotangent, routes, router_t, w_gate, w_up, w_down):
    d = tokens.shape[1]
    f = w_gate.shape[1]
    rows = GROUP * 8
    n = d // (NX * NL)
    cols = d // NX
    dma = pltpu.SemaphoreType.DMA
    return pl.pallas_call(
        layer_kernel,
        out_shape=[
            jax.ShapeDtypeStruct((3, n, f), F32),
            jax.ShapeDtypeStruct((2, 8, d), F32),
            jax.ShapeDtypeStruct((8, d), F32),
        ],
        in_specs=[ANY] * 7,
        out_specs=[ANY] * 3,
        scratch_shapes=[
            pltpu.VMEM((8, d), BF16),
            pltpu.VMEM((8, d), BF16),
            pltpu.VMEM(routes.shape, jnp.int32),
            pltpu.VMEM(router_t.shape, F32),
            pltpu.VMEM((3, NL, n, f), BF16),
            pltpu.VMEM((NL - 1, 8, cols), F32),
            pltpu.VMEM((3, n, f), F32),
            pltpu.VMEM((2, 8, d), F32),
            pltpu.VMEM((8, d), F32),
            pltpu.VMEM((NY, NZ, 2, 8, d), BF16),
            pltpu.VMEM((NY, NZ, 2, 8, d), BF16),
            pltpu.VMEM((GROUP, 8, 128), F32),
            pltpu.VMEM((8, 128), F32),
            pltpu.VMEM((GROUP, 1, rows), F32),
            pltpu.VMEM((1, rows), F32),
            pltpu.VMEM((3, d, f), BF16),
            pltpu.VMEM((rows, f), F32),
            pltpu.VMEM((rows, f), F32),
            pltpu.VMEM((rows, f), F32),
            pltpu.VMEM((NX, 3, rows, f), BF16),
            pltpu.VMEM((8, rows), F32),
            pltpu.VMEM((2, NY, NZ, 2, 8, d), BF16),
            pltpu.VMEM((2, NY, NZ, 8, d), BF16),
            pltpu.VMEM((2, NY, NZ, 8, d), BF16),
            pltpu.VMEM((2, NZ, 8, d), BF16),
            pltpu.VMEM((2, 2, NZ, 8, d), BF16),
            pltpu.VMEM((2, NZ, 8, d), BF16),
            pltpu.VMEM((2, 8, d), BF16),
            pltpu.VMEM((2, 2, 8, d), BF16),
            pltpu.VMEM((2, 8, d), BF16),
            pltpu.VMEM((3, NL, n, f), BF16),
            pltpu.VMEM((2, NX - 1, NY, NZ, 2, 8, cols), BF16),
            pltpu.VMEM((3, n, f), BF16),
            pltpu.VMEM((NX + 3, 8, cols), F32),
            pltpu.VMEM((8, cols), F32),
            pltpu.VMEM((8, cols), F32),
            dma((4,)), dma((5,)), dma((3,)), dma((2,)), dma((2, 8)), dma((2,)),
            dma, dma((8,)), dma, dma((8,)), dma((2,)),
            dma, dma((2, NY)), dma, dma((2, 2, NZ)), dma, dma((2, 2)),
            dma, dma((2,)), dma, dma((2,)),
            dma, dma((3, 2)), dma((3,)), dma, dma((3, 3)), dma((3,)), dma((3,)), dma((3,)),
        ],
        compiler_params=pltpu.CompilerParams(collective_id=0, has_side_effects=True),
        name="moe_layer",
    )(tokens, cotangent, routes, router_t, w_gate, w_up, w_down)


def finish_kernel(w, t, g, mo, to, go, o0, o1, o2):
    mo[...] = t[0].astype(BF16)
    to[...] = t[1].astype(BF16)
    go[...] = g[...]
    o0[...] = w[1]
    o1[...] = w[2]
    o2[...] = w[0]


def finish(w, t, g):
    grad = jax.ShapeDtypeStruct(w.shape[1:], F32)
    token = jax.ShapeDtypeStruct(t.shape[1:], BF16)
    return pl.pallas_call(
        finish_kernel,
        out_shape=[token, token, jax.ShapeDtypeStruct(g.shape, F32), grad, grad, grad],
        in_specs=[VMEM] * 3,
        out_specs=[VMEM] * 6,
        name="finish",
    )(w, t, g)


def local(tokens, routes, router, w_gate, w_up, w_down, cotangent):
    parts = layer(tokens, cotangent, routes, router.T, w_gate, w_up, w_down)
    mixed, grad_tokens, grad_router, grad_gate, grad_up, grad_down = finish(*parts)
    return (mixed, grad_tokens, grad_router.T, grad_gate, grad_up, grad_down)


def solution(mesh):
    return jax.shard_map(
        local,
        mesh=mesh,
        in_specs=(
            P(("dp", "expert"), None),
            P(("dp", "expert"), None),
            P(),
            P(None, "expert"),
            P(None, "expert"),
            P(None, "expert"),
            P(("dp", "expert"), None),
        ),
        out_specs=(
            P(("dp", "expert"), None),
            P(("dp", "expert"), None),
            P(),
            P("dp", "expert"),
            P("dp", "expert"),
            P("dp", "expert"),
        ),
        check_vma=False,
    )
```

```python
import jax
import jax.numpy as jnp
from jax import lax
from jax.experimental import pallas as pl
from jax.experimental.pallas import tpu as pltpu
from jax.sharding import PartitionSpec as P

NY = 4
NZ = 4
NX = 4
NL = 4
GROUP = 2 * NY * NZ
MESH = pl.DeviceIdType.MESH
VMEM = pl.BlockSpec(memory_space=pltpu.VMEM)
ANY = pl.BlockSpec(memory_space=pl.ANY)
F32 = jnp.float32
BF16 = jnp.bfloat16


def member(y, zh, core):
    return (lax.rem(y, NY) * NZ + lax.rem(zh, NZ)) * 2 + core


def dot(a, b, contract):
    return lax.dot_general(a, b, (contract, ((), ())), preferred_element_type=F32)


def thirds(a):
    one = a.astype(BF16).astype(F32)
    two = (a - one).astype(BF16).astype(F32)
    return jnp.concatenate([one, two, a - one - two], axis=0).astype(BF16)


def regroup(a):
    n = a.shape[0] // 3
    return a[:n] + a[n : 2 * n] + a[2 * n :]


def layer_kernel(x_hbm, c_hbm, routes_hbm, rt_hbm, wg_hbm, wu_hbm, wd_hbm,
                 wo_hbm, to_hbm, go_hbm,
                 x_ref, c_ref, routes_ref, rt, zo, gz, wo, to, gout,
                 xg, cg, mg, m_ref, pg, prow, wts, gate_pre, up_pre, pull, acts, lt,
                 part, cbuf, q, s1, fy, r, s1z, fz, r2,
                 dw, slices, aid, gx, gsum, gtot,
                 isem, osem, wsem, as_, ar, al, ms, mr, ps, pr, ml, cs, cr, ys, yr, zs, zr,
                 es, er, ts, tr, xs, xr, vr, us, ur, hr, gs, gr):
    j = lax.axis_index("expert")
    core = lax.rem(j, 2)
    zh = lax.rem(lax.div(j, 2), NZ)
    y = lax.div(j, 2 * NZ)
    dev = lax.axis_index("dp")
    x, zl = lax.div(dev, NL), lax.rem(dev, NL)
    d = x_ref.shape[1]
    rows = GROUP * 8

    def place(xx, zz):
        return lax.rem(xx, NX) * NL + lax.rem(zz, NL)

    def at(dy, dz):
        return member(y + dy, zh + dz, core)

    twin = member(y, zh, 1 - core)
    z_up, z_down, y_up, y_down = at(0, 1), at(0, 3), at(1, 0), at(3, 0)
    x_up, x_down = place(x + 1, zl), place(x + 3, zl)

    reads = [pltpu.make_async_copy(src, dst, isem.at[i])
             for i, (src, dst) in enumerate(((x_hbm, x_ref), (c_hbm, c_ref),
                                             (routes_hbm, routes_ref), (rt_hbm, rt)))]
    for copy in reads:
        copy.start()
    loads = [pltpu.make_async_copy(w, wts.at[i], wsem.at[i])
             for i, w in enumerate((wg_hbm, wu_hbm, wd_hbm))]
    for copy in loads:
        copy.start()

    barrier = pltpu.get_barrier_semaphore()
    near = [at(0, 1), at(0, 3), at(1, 0), at(2, 0), at(3, 0), twin]
    wide = [place(x + k, zl) for k in (1, 2, 3)] + [place(x, zl + k) for k in (1, 2, 3)]
    for peer in near:
        pl.semaphore_signal(barrier, inc=1, device_id={"expert": peer}, device_id_type=MESH)
    for peer in wide:
        pl.semaphore_signal(barrier, inc=1, device_id={"dp": peer}, device_id_type=MESH)
    for copy in reads:
        copy.wait()
    lanes = lax.broadcasted_iota(jnp.int32, m_ref.shape, 1)
    m_ref[...] = sum((routes_ref[:, k : k + 1] == lanes).astype(F32)
                     for k in range(routes_ref.shape[1]))
    pl.semaphore_wait(barrier, len(near) + len(wide))


    def remote(src, dst, send_sem, recv_sem, axis, target):
        return pltpu.make_async_remote_copy(
            src_ref=src, dst_ref=dst, send_sem=send_sem, recv_sem=recv_sem,
            device_id={axis: target}, device_id_type=MESH,
        )

    def go_on(*args):
        remote(*args).start()

    def landed(ref, sem):
        remote(ref, ref, sem, sem, "expert", twin).wait_recv()

    def gone(ref, sem):
        remote(ref, ref, sem, sem, "expert", twin).wait_send()

    ins, outs = (x_ref, c_ref), (xg, cg)
    three = cbuf.at[0, 0, pl.ds(0, 3)]

    def send(a, dy, dz, target, sem, own=False):
        block = lax.rem(y + dy, NY), lax.rem(zh + dz, NZ), core
        go_on(ins[a] if own else outs[a].at[block], outs[a].at[block],
              as_.at[a], ar.at[a, sem], "expert", target)

    def arrive_twin(a):
        landed(outs[a].at[:, :, 1 - core], ar.at[a, 7])

    def spread(a, dz, own=False):
        for target in (y_up, y_down, at(2, 0)):
            send(a, 0, dz, target, 3 + dz, own)
        send(a, 0, dz, twin, 7, own)

    def from_z(a, dz):
        zz = lax.rem(zh + dz, NZ)
        landed(outs[a].at[y, zz, core], ar.at[a, dz - 1])
        if dz != 2:
            ref = outs[a].at[y, zz, core, :, pl.ds((dz - 1) // 2 * (d // 2), d // 2)]
            go_on(ref, ref, as_.at[a], ar.at[a, 1], "expert", z_up if dz == 3 else z_down)
        spread(a, dz)

    def from_y(a, dz):
        landed(three, ar.at[a, 3 + dz])
        for dy in (3, 1, 2):
            send(a, dy, dz, twin, 7)

    cols = d // NX

    def lane(xx):
        return pl.ds(pl.multiple_of(lax.rem(xx, NX) * cols, cols), cols)

    def slice_out(a, dz):
        zz = lax.rem(zh + dz, NZ)
        for k in (2, 1, 3):
            go_on(outs[a].at[:, zz, core, :, lane(x + k)], slices.at[a, k - 1, :, zz, core],
                  es, er.at[a], "dp", place(x + k, zl))

    def slice_twin(a):
        ref = slices.at[a, :, :, :, core]
        landed(ref, er.at[a])
        go_on(ref, ref, ts, tr.at[a], "expert", twin)

    def slice_in(a):
        landed(slices.at[a, :, :, :, 1 - core], tr.at[a])

    class Small:
        def __init__(self, src, out, ssem, rsem, local):
            self.src, self.out, self.ssem, self.rsem = src, out, ssem, rsem
            self.keep = pltpu.make_async_copy(src, out.at[j], local)

        def send(self, block, target, sem, own=False):
            go_on(self.src if own else self.out.at[block], self.out.at[block],
                  self.ssem, self.rsem.at[sem], "expert", target)

        def spread(self, dz, own=False):
            for target in (y_up, y_down, at(2, 0)):
                self.send(at(0, dz), target, 3 + dz, own)
            self.send(at(0, dz), twin, 7, own)

        def first(self):
            for k in (1, 3):
                self.send(j, at(0, k), 3 - k, True)
            self.spread(0, True)
            self.keep.start()

        def second(self, *sides):
            for dz in sides:
                landed(self.out.at[at(0, dz)], self.rsem.at[dz - 1])
                if dz == 3:
                    self.send(at(0, dz), z_up, 1)
                self.spread(dz)

        def third(self):
            for dz in (0, 1, 3, 2):
                landed(self.out.at[pl.ds(0, 3)], self.rsem.at[3 + dz])
                for dy in (1, 3, 2):
                    self.send(at(dy, dz), twin, 7)

        def last(self):
            self.keep.wait()
            landed(self.out.at[pl.ds(0, NY * NZ)], self.rsem.at[7])

        def done(self):
            gone(self.out.at[pl.ds(0, GROUP - 1)], self.ssem)

    marks = Small(m_ref, mg, ms, mr, ml.at[0])
    pulls = Small(prow, pg, ps, pr, ml.at[1])

    for a in range(2):
        for k in (1, 3):
            send(a, 0, 0, at(0, k), 3 - k, True)
        if a == 0:
            marks.first()
    for a in range(2):
        spread(a, 0, True)
    held = [pltpu.make_async_copy(ins[a], outs[a].at[y, zh, core], al.at[a]) for a in range(2)]
    for copy in held:
        copy.start()
    def all_y(a, dz):
        from_y(a, dz)
        slice_out(a, dz)

    for copy in loads + held:
        copy.wait()
    all_y(0, 0)
    for dz in (3, 1):
        from_z(0, dz)
    marks.second(3, 1)
    from_z(0, 2)
    all_y(1, 0)
    for dz in (3, 1):
        from_z(1, dz)
    for dz in (3, 1):
        all_y(0, dz)
    marks.second(2)
    all_y(0, 2)
    marks.third()
    from_z(1, 2)
    arrive_twin(0)

    xv, cv = xg.reshape(rows, d), cg.reshape(rows, d)
    gate_pre[...] = dot(xv[...], wts[0], ((1,), (0,)))
    up_pre[...] = dot(xv[...], wts[1], ((1,), (0,)))
    logits = regroup(dot(thirds(rt[...]), xv[...], ((1,), (1,))))
    affinity = jax.nn.sigmoid(logits)
    for dz in (3, 1):
        all_y(1, dz)
    marks.last()
    mask = jnp.transpose(mg.reshape(rows, 128)[...])[:8]
    denominator = jnp.sum(affinity * mask, axis=0, keepdims=True)
    gates = mask * affinity / denominator
    wide_gates = jnp.transpose(jnp.concatenate([gates, jnp.zeros((120, rows), F32)], axis=0))
    mine = lax.broadcasted_iota(jnp.int32, wide_gates.shape, 1) == lax.div(j, 4)
    gate = jnp.sum(jnp.where(mine, wide_gates, 0.0), axis=1, keepdims=True)
    hs, dg, du = acts.at[0, 0], acts.at[0, 1], acts.at[0, 2]
    hs[...] = (gate * (gate_pre[...] * jax.nn.sigmoid(gate_pre[...]) * up_pre[...])).astype(BF16)

    def hidden_back():
        pull[...] = dot(cv[...], wts[2], ((1,), (0,)))
        sigma = jax.nn.sigmoid(gate_pre[...])
        silu = gate_pre[...] * sigma
        hidden = silu * up_pre[...]
        prow[...] = jnp.sum(jnp.transpose(hidden * pull[...]), axis=0, keepdims=True)
        hidden_grad = gate * pull[...]
        dg[...] = (hidden_grad * up_pre[...] * sigma
                   * (1.0 + gate_pre[...] * (1.0 - sigma))).astype(BF16)
        du[...] = (hidden_grad * silu).astype(BF16)

    half = rows // 2
    ends = pl.ds(0, half), pl.ds(half, half)

    def acts_first(p):
        go_on(acts.at[0, p], acts.at[1, p], xs, xr.at[p, 0], "dp", x_up)
        go_on(acts.at[0, p], acts.at[3, p], xs, xr.at[p, 1], "dp", x_down)

    def acts_second(p):
        for h in range(2):
            landed(acts.at[(1, 3)[h], p], xr.at[p, h])
            go_on(acts.at[(1, 3)[h], p, ends[h]], acts.at[2, p, ends[h]], xs,
                  vr.at[p], "dp", (x_up, x_down)[h])

    def weight_rows(p):
        landed(acts.at[2, p], vr.at[p])
        a = 0 if p else 1
        value = dot((cv, xv)[p > 0][:, lane(x)], acts[0, p], ((0,), (0,)))
        for k in (1, 2, 3):
            other = slices.at[a, k - 1].reshape(rows, cols)
            value = value + dot(other[...], acts[k, p], ((0,), (0,)))
        dw[p] = value.astype(BF16).reshape(dw.shape[1:])

    writes = []

    def write(src, dst, i):
        copy = pltpu.make_async_copy(src, dst, osem.at[i])
        copy.start()
        writes.append(copy)

    is_end = jnp.logical_or(zl == 0, zl == NL - 1)

    def hop(p, k, to_aid):
        shard = dw.at[p, lax.rem(zl + k, NL)]
        if to_aid:
            return remote(shard, aid.at[p], us, hr.at[p], "dp", place(x, zl + NL - k))
        return remote(shard, zo.at[p, k], us, ur.at[p, k - 1], "dp",
                      place(x, zl + k))

    def across_first(p):
        for k, end in ((3, 0), (1, NL - 1)):
            @pl.when(zl == end)
            def _():
                hop(p, k, True).start()

            @pl.when(zl != end)
            def _():
                hop(p, k, False).start()

        @pl.when(is_end)
        def _():
            hop(p, 2, False).start()

        zo[p, 0] = dw[p, zl]

        @pl.when(zl == 0)
        def _():
            zo[p, 1] = jnp.zeros(zo.shape[2:], BF16)

        @pl.when(zl == NL - 1)
        def _():
            zo[p, 3] = jnp.zeros(zo.shape[2:], BF16)

    def across_second(p):
        @pl.when(jnp.logical_not(is_end))
        def _():
            landed(aid.at[p], hr.at[p])
            aid[p] = (dw[p, lax.rem(zl + 2, NL)].astype(F32) + aid[p].astype(F32)).astype(BF16)
            remote(aid.at[p], zo.at[p, 2], us, ur.at[p, 1], "dp",
                   place(x, zl + 2)).start()

    def across_last(p):
        landed(zo.at[p, 2], ur.at[p, 1])
        for k, none in ((3, NL - 1), (1, 0)):
            @pl.when(zl != none)
            def _():
                landed(zo.at[p, k], ur.at[p, k - 1])

        wo[p] = (zo[p, 0].astype(F32) + zo[p, 1].astype(F32)
                 + zo[p, 2].astype(F32) + zo[p, 3].astype(F32))
        write(wo.at[p], wo_hbm.at[p], p)

    def start_core(a):
        for dy in (2, 1, 3, 0):
            yy = lax.rem(y + dy, NY)
            go_on(part.at[a, yy, :, 1 - core], cbuf.at[a, yy], cs, cr.at[a, yy],
                  "expert", twin)

    def add_core(a, dy):
        yy = lax.rem(y + dy, NY)
        landed(cbuf.at[a, yy], cr.at[a, yy])

        @pl.loop(0, NZ)
        def _(k):
            q[a, yy, k] = (part[a, yy, k, core].astype(F32)
                           + cbuf[a, yy, k].astype(F32)).astype(BF16)

    y1, y2, y3 = lax.rem(y + 1, NY), lax.rem(y + 2, NY), lax.rem(y + 3, NY)

    def row(k):
        return lax.rem(zh + k, NZ)

    def y_start(a, k):
        zz = row(k)
        go_on(q.at[a, y2, zz], s1.at[a, zz], ys, yr.at[a, 0, k], "expert",
              (y_up, y_down)[a])

    def y_first(a):
        for dy in (2, 1, 3):
            add_core(a, dy)
        y_start(a, 2)
        y_start(a, 1)
        for k in (2, 1, 3, 0):
            go_on(q.at[a, (y3, y1)[a], row(k)], fy.at[a, 1 - a, row(k)], ys,
                  yr.at[a, 1, k], "expert", (y_down, y_up)[a])
        add_core(a, 0)

    def y_pass(a, k):
        zz = row(k)
        landed(s1.at[a, zz], yr.at[a, 0, k])
        s1[a, zz] = (q[a, (y1, y3)[a], zz].astype(F32) + s1[a, zz].astype(F32)).astype(BF16)
        go_on(s1.at[a, zz], fy.at[a, a, zz], ys, yr.at[a, 1, k], "expert",
              (y_up, y_down)[a])

    h1, h2, h3 = lax.rem(zh + 1, NZ), lax.rem(zh + 2, NZ), lax.rem(zh + 3, NZ)

    def y_end(a, k):
        zz = row(k)
        landed(fy.at[a, :, zz], yr.at[a, 1, k])
        r[a, zz] = (q[a, y, zz].astype(F32) + fy[a, 0, zz].astype(F32)
                    + fy[a, 1, zz].astype(F32)).astype(BF16)
        if k == 2:
            go_on(r.at[a, zz], s1z.at[a], zs, zr.at[a, 0], "expert", (z_up, z_down)[a])
        if k == (3, 1)[a]:
            go_on(r.at[a, zz], fz.at[a, 1 - a], zs, zr.at[a, 1], "expert",
                  (z_down, z_up)[a])

    def z_second(a):
        landed(s1z.at[a], zr.at[a, 0])
        r2[a] = (r[a, (h1, h3)[a]].astype(F32) + s1z[a].astype(F32)).astype(BF16)
        go_on(r2.at[a], fz.at[a, a], zs, zr.at[a, 1], "expert",
              (z_up, z_down)[a])

    def z_third(a):
        landed(fz.at[a], zr.at[a, 1])
        return r[a, zh].astype(F32) + fz[a, 0].astype(F32) + fz[a, 1].astype(F32)

    def router_first():
        sums = []
        for e in range(8):
            sums.append(pg[4 * e] + pg[4 * e + 1] + pg[4 * e + 2] + pg[4 * e + 3])
        full = jnp.concatenate(sums, axis=0)
        mean = jnp.sum(gates * full, axis=0, keepdims=True)
        lt[...] = mask * (full - mean) / denominator * affinity * (1.0 - affinity)
        value = regroup(dot(thirds(lt[...]), xv[...], ((1,), (0,))))
        for k in range(NX):
            gx[k] = value[:, k * cols : (k + 1) * cols]
        for k in (1, 2, 3):
            go_on(gx.at[lax.rem(x + k, NX)], gx.at[NX + k - 1], gs.at[0],
                  gr.at[0], "dp", place(x + k, zl))

    def router_second():
        landed(gx.at[pl.ds(NX, 3)], gr.at[0])
        gsum[...] = gx[x] + gx[NX] + gx[NX + 1] + gx[NX + 2]
        for k in (1, 2, 3):
            go_on(gsum, gz.at[k - 1], gs.at[1], gr.at[1], "dp", place(x, zl + k))

    def router_third():
        landed(gz, gr.at[1])
        gtot[...] = gsum[...] + gz[0] + gz[1] + gz[2]
        for k in (1, 2, 3):
            go_on(gtot, gout.at[:, lane(x)], gs.at[2], gr.at[2], "dp",
                  place(x + k, zl))
        gout[:, lane(x)] = gtot[...]

    def router_last():
        landed(gz, gr.at[2])

    acts_first(0)
    part.reshape(2, rows, d)[0] = dot(hs[...], wts[2], ((1,), (1,))).astype(BF16)
    start_core(0)
    all_y(1, 2)
    y_first(0)
    y_pass(0, 2)
    y_start(0, 3)
    acts_second(0)
    y_pass(0, 1)
    y_start(0, 0)
    arrive_twin(1)
    hidden_back()
    acts_first(1)
    acts_first(2)
    pulls.first()
    y_pass(0, 3)
    y_end(0, 2)
    part.reshape(2, rows, d)[1] = (dot(dg[...], wts[0], ((1,), (1,)))
                                   + dot(du[...], wts[1], ((1,), (1,)))).astype(BF16)
    start_core(1)
    y_pass(0, 0)
    y_end(0, 1)
    y_first(1)
    pulls.second(3, 1)
    slice_twin(1)
    y_end(0, 3)
    slice_in(1)
    weight_rows(0)
    across_first(0)
    y_pass(1, 2)
    y_start(1, 3)
    y_end(0, 0)
    slice_twin(0)
    acts_second(1)
    y_pass(1, 1)
    y_start(1, 0)
    z_second(0)
    y_end(1, 2)
    pulls.second(2)
    y_pass(1, 3)
    acts_second(2)
    y_pass(1, 0)
    y_end(1, 1)
    pulls.third()
    slice_in(0)
    weight_rows(1)
    across_first(1)
    y_end(1, 3)
    pulls.last()
    router_first()
    across_second(0)
    weight_rows(2)
    router_second()
    across_first(2)
    y_end(1, 0)
    z_second(1)
    across_second(1)
    across_second(2)
    router_third()
    to[0] = z_third(0)
    total = z_third(1)
    ours = lax.broadcasted_iota(jnp.int32, (8, rows), 0) + 8 * j
    pick = lax.broadcasted_iota(jnp.int32, (8, rows), 1) == ours
    for e in range(8):
        weight = jnp.sum(jnp.where(pick, lt[e : e + 1, :], 0.0), axis=1, keepdims=True)
        total = total + weight * rt[e : e + 1, :]
    to[1] = total
    write(to, to_hbm, 3)
    router_last()
    write(gout, go_hbm, 4)
    for p in range(3):
        across_last(p)
    for a in range(2):
        gone(outs[a].reshape(GROUP, 8, d).at[pl.ds(0, GROUP - 1)], as_.at[a])
    marks.done()
    pulls.done()
    gone(slices.at[:, :, :, :, 0], es)
    gone(slices.at[:, :, :, :, 0], ts)
    gone(cbuf, cs)
    gone(cbuf.at[:, pl.ds(0, 3)], ys)
    gone(cbuf.at[:, 0, pl.ds(0, 3)], zs)
    gone(acts.at[pl.ds(0, 3)], xs)
    gone(zo.at[:, pl.ds(0, 3)], us)
    for i in range(3):
        gone(gz, gs.at[i])
    for copy in writes:
        copy.wait()


def layer(tokens, cotangent, routes, router_t, w_gate, w_up, w_down):
    d = tokens.shape[1]
    f = w_gate.shape[1]
    rows = GROUP * 8
    n = d // (NX * NL)
    cols = d // NX
    dma = pltpu.SemaphoreType.DMA
    return pl.pallas_call(
        layer_kernel,
        out_shape=[
            jax.ShapeDtypeStruct((3, n, f), F32),
            jax.ShapeDtypeStruct((2, 8, d), F32),
            jax.ShapeDtypeStruct((8, d), F32),
        ],
        in_specs=[ANY] * 7,
        out_specs=[ANY] * 3,
        scratch_shapes=[
            pltpu.VMEM((8, d), BF16),
            pltpu.VMEM((8, d), BF16),
            pltpu.VMEM(routes.shape, jnp.int32),
            pltpu.VMEM(router_t.shape, F32),
            pltpu.VMEM((3, NL, n, f), BF16),
            pltpu.VMEM((NL - 1, 8, cols), F32),
            pltpu.VMEM((3, n, f), F32),
            pltpu.VMEM((2, 8, d), F32),
            pltpu.VMEM((8, d), F32),
            pltpu.VMEM((NY, NZ, 2, 8, d), BF16),
            pltpu.VMEM((NY, NZ, 2, 8, d), BF16),
            pltpu.VMEM((GROUP, 8, 128), F32),
            pltpu.VMEM((8, 128), F32),
            pltpu.VMEM((GROUP, 1, rows), F32),
            pltpu.VMEM((1, rows), F32),
            pltpu.VMEM((3, d, f), BF16),
            pltpu.VMEM((rows, f), F32),
            pltpu.VMEM((rows, f), F32),
            pltpu.VMEM((rows, f), F32),
            pltpu.VMEM((NX, 3, rows, f), BF16),
            pltpu.VMEM((8, rows), F32),
            pltpu.VMEM((2, NY, NZ, 2, 8, d), BF16),
            pltpu.VMEM((2, NY, NZ, 8, d), BF16),
            pltpu.VMEM((2, NY, NZ, 8, d), BF16),
            pltpu.VMEM((2, NZ, 8, d), BF16),
            pltpu.VMEM((2, 2, NZ, 8, d), BF16),
            pltpu.VMEM((2, NZ, 8, d), BF16),
            pltpu.VMEM((2, 8, d), BF16),
            pltpu.VMEM((2, 2, 8, d), BF16),
            pltpu.VMEM((2, 8, d), BF16),
            pltpu.VMEM((3, NL, n, f), BF16),
            pltpu.VMEM((2, NX - 1, NY, NZ, 2, 8, cols), BF16),
            pltpu.VMEM((3, n, f), BF16),
            pltpu.VMEM((NX + 3, 8, cols), F32),
            pltpu.VMEM((8, cols), F32),
            pltpu.VMEM((8, cols), F32),
            dma((4,)), dma((5,)), dma((3,)), dma((2,)), dma((2, 8)), dma((2,)),
            dma, dma((8,)), dma, dma((8,)), dma((2,)),
            dma, dma((2, NY)), dma, dma((2, 2, NZ)), dma, dma((2, 2)),
            dma, dma((2,)), dma, dma((2,)),
            dma, dma((3, 2)), dma((3,)), dma, dma((3, 3)), dma((3,)), dma((3,)), dma((3,)),
        ],
        compiler_params=pltpu.CompilerParams(collective_id=0, has_side_effects=True),
        name="moe_layer",
    )(tokens, cotangent, routes, router_t, w_gate, w_up, w_down)


def finish_kernel(w, t, g, mo, to, go, o0, o1, o2):
    mo[...] = t[0].astype(BF16)
    to[...] = t[1].astype(BF16)
    go[...] = g[...]
    o0[...] = w[1]
    o1[...] = w[2]
    o2[...] = w[0]


def finish(w, t, g):
    grad = jax.ShapeDtypeStruct(w.shape[1:], F32)
    token = jax.ShapeDtypeStruct(t.shape[1:], BF16)
    return pl.pallas_call(
        finish_kernel,
        out_shape=[token, token, jax.ShapeDtypeStruct(g.shape, F32), grad, grad, grad],
        in_specs=[VMEM] * 3,
        out_specs=[VMEM] * 6,
        name="finish",
    )(w, t, g)


def local(tokens, routes, router, w_gate, w_up, w_down, cotangent):
    parts = layer(tokens, cotangent, routes, router.T, w_gate, w_up, w_down)
    mixed, grad_tokens, grad_router, grad_gate, grad_up, grad_down = finish(*parts)
    return (mixed, grad_tokens, grad_router.T, grad_gate, grad_up, grad_down)


def solution(mesh):
    return jax.shard_map(
        local,
        mesh=mesh,
        in_specs=(
            P(("dp", "expert"), None),
            P(("dp", "expert"), None),
            P(),
            P(None, "expert"),
            P(None, "expert"),
            P(None, "expert"),
            P(("dp", "expert"), None),
        ),
        out_specs=(
            P(("dp", "expert"), None),
            P(("dp", "expert"), None),
            P(),
            P("dp", "expert"),
            P("dp", "expert"),
            P("dp", "expert"),
        ),
        check_vma=False,
    )
```

```python
import jax
import jax.numpy as jnp
from jax import lax
from jax.experimental import pallas as pl
from jax.experimental.pallas import tpu as pltpu
from jax.sharding import PartitionSpec as P

NY = 4
NZ = 4
NX = 4
NL = 4
GROUP = 2 * NY * NZ
MESH = pl.DeviceIdType.MESH
VMEM = pl.BlockSpec(memory_space=pltpu.VMEM)
ANY = pl.BlockSpec(memory_space=pl.ANY)
F32 = jnp.float32
BF16 = jnp.bfloat16


def member(y, zh, core):
    return (lax.rem(y, NY) * NZ + lax.rem(zh, NZ)) * 2 + core


def dot(a, b, contract):
    return lax.dot_general(a, b, (contract, ((), ())), preferred_element_type=F32)


def thirds(a):
    one = a.astype(BF16).astype(F32)
    two = (a - one).astype(BF16).astype(F32)
    return jnp.concatenate([one, two, a - one - two], axis=0).astype(BF16)


def regroup(a):
    n = a.shape[0] // 3
    return a[:n] + a[n : 2 * n] + a[2 * n :]


def layer_kernel(x_hbm, c_hbm, routes_hbm, rt_hbm, wg_hbm, wu_hbm, wd_hbm,
                 wo_hbm, to_hbm, go_hbm,
                 x_ref, c_ref, routes_ref, rt, zo, gz, wo, to, gout,
                 xg, cg, mg, m_ref, pg, prow, wts, gate_pre, up_pre, pull, acts, lt,
                 part, cbuf, q, s1, fy, r, s1z, fz, r2,
                 dw, slices, aid, gx, gsum, gtot,
                 isem, osem, wsem, as_, ar, al, ms, mr, ps, pr, ml, cs, cr, ys, yr, zs, zr,
                 es, er, ts, tr, xs, xr, vr, us, ur, hr, gs, gr):
    j = lax.axis_index("expert")
    core = lax.rem(j, 2)
    zh = lax.rem(lax.div(j, 2), NZ)
    y = lax.div(j, 2 * NZ)
    dev = lax.axis_index("dp")
    x, zl = lax.div(dev, NL), lax.rem(dev, NL)
    d = x_ref.shape[1]
    rows = GROUP * 8

    def place(xx, zz):
        return lax.rem(xx, NX) * NL + lax.rem(zz, NL)

    def at(dy, dz):
        return member(y + dy, zh + dz, core)

    twin = member(y, zh, 1 - core)
    z_up, z_down, y_up, y_down = at(0, 1), at(0, 3), at(1, 0), at(3, 0)
    x_up, x_down = place(x + 1, zl), place(x + 3, zl)

    reads = [pltpu.make_async_copy(src, dst, isem.at[i])
             for i, (src, dst) in enumerate(((x_hbm, x_ref), (c_hbm, c_ref),
                                             (routes_hbm, routes_ref), (rt_hbm, rt)))]
    for copy in reads:
        copy.start()
    loads = [pltpu.make_async_copy(w, wts.at[i], wsem.at[i])
             for i, w in enumerate((wg_hbm, wu_hbm, wd_hbm))]
    for copy in loads:
        copy.start()

    barrier = pltpu.get_barrier_semaphore()
    near = [at(0, 1), at(0, 3), at(1, 0), at(2, 0), at(3, 0), twin]
    wide = [place(x + k, zl) for k in (1, 2, 3)] + [place(x, zl + k) for k in (1, 2, 3)]
    for peer in near:
        pl.semaphore_signal(barrier, inc=1, device_id={"expert": peer}, device_id_type=MESH)
    for peer in wide:
        pl.semaphore_signal(barrier, inc=1, device_id={"dp": peer}, device_id_type=MESH)
    for copy in reads:
        copy.wait()
    lanes = lax.broadcasted_iota(jnp.int32, m_ref.shape, 1)
    m_ref[...] = sum((routes_ref[:, k : k + 1] == lanes).astype(F32)
                     for k in range(routes_ref.shape[1]))
    pl.semaphore_wait(barrier, len(near) + len(wide))


    def remote(src, dst, send_sem, recv_sem, axis, target):
        return pltpu.make_async_remote_copy(
            src_ref=src, dst_ref=dst, send_sem=send_sem, recv_sem=recv_sem,
            device_id={axis: target}, device_id_type=MESH,
        )

    def go_on(*args):
        remote(*args).start()

    def landed(ref, sem):
        remote(ref, ref, sem, sem, "expert", twin).wait_recv()

    def gone(ref, sem):
        remote(ref, ref, sem, sem, "expert", twin).wait_send()

    ins, outs = (x_ref, c_ref), (xg, cg)
    three = cbuf.at[0, 0, pl.ds(0, 3)]

    def send(a, dy, dz, target, sem, own=False):
        block = lax.rem(y + dy, NY), lax.rem(zh + dz, NZ), core
        go_on(ins[a] if own else outs[a].at[block], outs[a].at[block],
              as_.at[a], ar.at[a, sem], "expert", target)

    def arrive_twin(a):
        landed(outs[a].at[:, :, 1 - core], ar.at[a, 7])

    def spread(a, dz, own=False):
        for target in (y_up, y_down, at(2, 0)):
            send(a, 0, dz, target, 3 + dz, own)
        send(a, 0, dz, twin, 7, own)

    def from_z(a, dz):
        zz = lax.rem(zh + dz, NZ)
        landed(outs[a].at[y, zz, core], ar.at[a, dz - 1])
        if dz != 2:
            ref = outs[a].at[y, zz, core, :, pl.ds((dz - 1) // 2 * (d // 2), d // 2)]
            go_on(ref, ref, as_.at[a], ar.at[a, 1], "expert", z_up if dz == 3 else z_down)
        spread(a, dz)

    def from_y(a, dz):
        landed(three, ar.at[a, 3 + dz])
        for dy in (3, 1, 2):
            send(a, dy, dz, twin, 7)

    cols = d // NX

    def lane(xx):
        return pl.ds(pl.multiple_of(lax.rem(xx, NX) * cols, cols), cols)

    def slice_out(a, dz):
        zz = lax.rem(zh + dz, NZ)
        for k in (2, 1, 3):
            go_on(outs[a].at[:, zz, core, :, lane(x + k)], slices.at[a, k - 1, :, zz, core],
                  es, er.at[a], "dp", place(x + k, zl))

    def slice_twin(a):
        ref = slices.at[a, :, :, :, core]
        landed(ref, er.at[a])
        go_on(ref, ref, ts, tr.at[a], "expert", twin)

    def slice_in(a):
        landed(slices.at[a, :, :, :, 1 - core], tr.at[a])

    class Small:
        def __init__(self, src, out, ssem, rsem, local):
            self.src, self.out, self.ssem, self.rsem = src, out, ssem, rsem
            self.keep = pltpu.make_async_copy(src, out.at[j], local)

        def send(self, block, target, sem, own=False):
            go_on(self.src if own else self.out.at[block], self.out.at[block],
                  self.ssem, self.rsem.at[sem], "expert", target)

        def spread(self, dz, own=False):
            for target in (y_up, y_down, at(2, 0)):
                self.send(at(0, dz), target, 3 + dz, own)
            self.send(at(0, dz), twin, 7, own)

        def first(self):
            for k in (1, 3):
                self.send(j, at(0, k), 3 - k, True)
            self.spread(0, True)
            self.keep.start()

        def second(self, *sides):
            for dz in sides:
                landed(self.out.at[at(0, dz)], self.rsem.at[dz - 1])
                if dz == 3:
                    self.send(at(0, dz), z_up, 1)
                self.spread(dz)

        def third(self):
            for dz in (0, 1, 3, 2):
                landed(self.out.at[pl.ds(0, 3)], self.rsem.at[3 + dz])
                for dy in (1, 3, 2):
                    self.send(at(dy, dz), twin, 7)

        def last(self):
            self.keep.wait()
            landed(self.out.at[pl.ds(0, NY * NZ)], self.rsem.at[7])

        def done(self):
            gone(self.out.at[pl.ds(0, GROUP - 1)], self.ssem)

    marks = Small(m_ref, mg, ms, mr, ml.at[0])
    pulls = Small(prow, pg, ps, pr, ml.at[1])

    for a in range(2):
        for k in (1, 3):
            send(a, 0, 0, at(0, k), 3 - k, True)
        if a == 0:
            marks.first()
    for a in range(2):
        spread(a, 0, True)
    held = [pltpu.make_async_copy(ins[a], outs[a].at[y, zh, core], al.at[a]) for a in range(2)]
    for copy in held:
        copy.start()
    def all_y(a, dz):
        from_y(a, dz)
        slice_out(a, dz)

    for copy in loads + held:
        copy.wait()
    all_y(0, 0)
    for dz in (3, 1):
        from_z(0, dz)
    marks.second(3, 1)
    from_z(0, 2)
    all_y(1, 0)
    for dz in (3, 1):
        from_z(1, dz)
    for dz in (3, 1):
        all_y(0, dz)
    marks.second(2)
    all_y(0, 2)
    marks.third()
    from_z(1, 2)
    arrive_twin(0)

    xv, cv = xg.reshape(rows, d), cg.reshape(rows, d)
    gate_pre[...] = dot(xv[...], wts[0], ((1,), (0,)))
    up_pre[...] = dot(xv[...], wts[1], ((1,), (0,)))
    logits = regroup(dot(thirds(rt[...]), xv[...], ((1,), (1,))))
    affinity = jax.nn.sigmoid(logits)
    for dz in (3, 1):
        all_y(1, dz)
    marks.last()
    mask = jnp.transpose(mg.reshape(rows, 128)[...])[:8]
    denominator = jnp.sum(affinity * mask, axis=0, keepdims=True)
    gates = mask * affinity / denominator
    wide_gates = jnp.transpose(jnp.concatenate([gates, jnp.zeros((120, rows), F32)], axis=0))
    mine = lax.broadcasted_iota(jnp.int32, wide_gates.shape, 1) == lax.div(j, 4)
    gate = jnp.sum(jnp.where(mine, wide_gates, 0.0), axis=1, keepdims=True)
    hs, dg, du = acts.at[0, 0], acts.at[0, 1], acts.at[0, 2]
    hs[...] = (gate * (gate_pre[...] * jax.nn.sigmoid(gate_pre[...]) * up_pre[...])).astype(BF16)

    def hidden_back():
        pull[...] = dot(cv[...], wts[2], ((1,), (0,)))
        sigma = jax.nn.sigmoid(gate_pre[...])
        silu = gate_pre[...] * sigma
        hidden = silu * up_pre[...]
        prow[...] = jnp.sum(jnp.transpose(hidden * pull[...]), axis=0, keepdims=True)
        hidden_grad = gate * pull[...]
        dg[...] = (hidden_grad * up_pre[...] * sigma
                   * (1.0 + gate_pre[...] * (1.0 - sigma))).astype(BF16)
        du[...] = (hidden_grad * silu).astype(BF16)

    half = rows // 2
    ends = pl.ds(0, half), pl.ds(half, half)

    def acts_first(p):
        go_on(acts.at[0, p], acts.at[1, p], xs, xr.at[p, 0], "dp", x_up)
        go_on(acts.at[0, p], acts.at[3, p], xs, xr.at[p, 1], "dp", x_down)

    def acts_second(p):
        for h in range(2):
            landed(acts.at[(1, 3)[h], p], xr.at[p, h])
            go_on(acts.at[(1, 3)[h], p, ends[h]], acts.at[2, p, ends[h]], xs,
                  vr.at[p], "dp", (x_up, x_down)[h])

    def weight_rows(p):
        landed(acts.at[2, p], vr.at[p])
        a = 0 if p else 1
        value = dot((cv, xv)[p > 0][:, lane(x)], acts[0, p], ((0,), (0,)))
        for k in (1, 2, 3):
            other = slices.at[a, k - 1].reshape(rows, cols)
            value = value + dot(other[...], acts[k, p], ((0,), (0,)))
        dw[p] = value.astype(BF16).reshape(dw.shape[1:])

    writes = []

    def write(src, dst, i):
        copy = pltpu.make_async_copy(src, dst, osem.at[i])
        copy.start()
        writes.append(copy)

    is_end = jnp.logical_or(zl == 0, zl == NL - 1)

    def hop(p, k, to_aid):
        shard = dw.at[p, lax.rem(zl + k, NL)]
        if to_aid:
            return remote(shard, aid.at[p], us, hr.at[p], "dp", place(x, zl + NL - k))
        return remote(shard, zo.at[p, k], us, ur.at[p, k - 1], "dp",
                      place(x, zl + k))

    def across_first(p):
        zo[p, 0] = dw[p, zl]
        if p == 2:
            for k in (2, 1, 3):
                hop(p, k, False).start()
            return
        for k, end in ((3, 0), (1, NL - 1)):
            @pl.when(zl == end)
            def _():
                hop(p, k, True).start()

            @pl.when(zl != end)
            def _():
                hop(p, k, False).start()

        @pl.when(is_end)
        def _():
            hop(p, 2, False).start()

        @pl.when(zl == 0)
        def _():
            zo[p, 1] = jnp.zeros(zo.shape[2:], BF16)

        @pl.when(zl == NL - 1)
        def _():
            zo[p, 3] = jnp.zeros(zo.shape[2:], BF16)

    def across_second(p):
        @pl.when(jnp.logical_not(is_end))
        def _():
            landed(aid.at[p], hr.at[p])
            aid[p] = (dw[p, lax.rem(zl + 2, NL)].astype(F32) + aid[p].astype(F32)).astype(BF16)
            remote(aid.at[p], zo.at[p, 2], us, ur.at[p, 1], "dp",
                   place(x, zl + 2)).start()

    def across_last(p):
        landed(zo.at[p, 2], ur.at[p, 1])
        for k, none in ((3, NL - 1), (1, 0)):
            @pl.when(zl != (none if p < 2 else NL))
            def _():
                landed(zo.at[p, k], ur.at[p, k - 1])

        wo[p] = (zo[p, 0].astype(F32) + zo[p, 1].astype(F32)
                 + zo[p, 2].astype(F32) + zo[p, 3].astype(F32))
        write(wo.at[p], wo_hbm.at[p], p)

    def start_core(a):
        for dy in (2, 1, 3, 0):
            yy = lax.rem(y + dy, NY)
            go_on(part.at[a, yy, :, 1 - core], cbuf.at[a, yy], cs, cr.at[a, yy],
                  "expert", twin)

    def add_core(a, dy):
        yy = lax.rem(y + dy, NY)
        landed(cbuf.at[a, yy], cr.at[a, yy])

        @pl.loop(0, NZ)
        def _(k):
            q[a, yy, k] = (part[a, yy, k, core].astype(F32)
                           + cbuf[a, yy, k].astype(F32)).astype(BF16)

    y1, y2, y3 = lax.rem(y + 1, NY), lax.rem(y + 2, NY), lax.rem(y + 3, NY)

    def row(k):
        return lax.rem(zh + k, NZ)

    def y_start(a, k):
        zz = row(k)
        go_on(q.at[a, y2, zz], s1.at[a, zz], ys, yr.at[a, 0, k], "expert",
              (y_up, y_down)[a])

    def y_first(a):
        for dy in (2, 1, 3):
            add_core(a, dy)
        y_start(a, 2)
        y_start(a, 1)
        for k in (2, 1, 3, 0):
            go_on(q.at[a, (y3, y1)[a], row(k)], fy.at[a, 1 - a, row(k)], ys,
                  yr.at[a, 1, k], "expert", (y_down, y_up)[a])
        add_core(a, 0)

    def y_pass(a, k):
        zz = row(k)
        landed(s1.at[a, zz], yr.at[a, 0, k])
        s1[a, zz] = (q[a, (y1, y3)[a], zz].astype(F32) + s1[a, zz].astype(F32)).astype(BF16)
        go_on(s1.at[a, zz], fy.at[a, a, zz], ys, yr.at[a, 1, k], "expert",
              (y_up, y_down)[a])

    h1, h2, h3 = lax.rem(zh + 1, NZ), lax.rem(zh + 2, NZ), lax.rem(zh + 3, NZ)

    def y_end(a, k):
        zz = row(k)
        landed(fy.at[a, :, zz], yr.at[a, 1, k])
        r[a, zz] = (q[a, y, zz].astype(F32) + fy[a, 0, zz].astype(F32)
                    + fy[a, 1, zz].astype(F32)).astype(BF16)
        if k == 2:
            go_on(r.at[a, zz], s1z.at[a], zs, zr.at[a, 0], "expert", (z_up, z_down)[a])
        if k == (3, 1)[a]:
            go_on(r.at[a, zz], fz.at[a, 1 - a], zs, zr.at[a, 1], "expert",
                  (z_down, z_up)[a])

    def z_second(a):
        landed(s1z.at[a], zr.at[a, 0])
        r2[a] = (r[a, (h1, h3)[a]].astype(F32) + s1z[a].astype(F32)).astype(BF16)
        go_on(r2.at[a], fz.at[a, a], zs, zr.at[a, 1], "expert",
              (z_up, z_down)[a])

    def z_third(a):
        landed(fz.at[a], zr.at[a, 1])
        return r[a, zh].astype(F32) + fz[a, 0].astype(F32) + fz[a, 1].astype(F32)

    def router_first():
        sums = []
        for e in range(8):
            sums.append(pg[4 * e] + pg[4 * e + 1] + pg[4 * e + 2] + pg[4 * e + 3])
        full = jnp.concatenate(sums, axis=0)
        mean = jnp.sum(gates * full, axis=0, keepdims=True)
        lt[...] = mask * (full - mean) / denominator * affinity * (1.0 - affinity)
        value = regroup(dot(thirds(lt[...]), xv[...], ((1,), (0,))))
        for k in range(NX):
            gx[k] = value[:, k * cols : (k + 1) * cols]
        for k in (1, 2, 3):
            go_on(gx.at[lax.rem(x + k, NX)], gx.at[NX + k - 1], gs.at[0],
                  gr.at[0], "dp", place(x + k, zl))

    def router_second():
        landed(gx.at[pl.ds(NX, 3)], gr.at[0])
        gsum[...] = gx[x] + gx[NX] + gx[NX + 1] + gx[NX + 2]
        for k in (1, 2, 3):
            go_on(gsum, gz.at[k - 1], gs.at[1], gr.at[1], "dp", place(x, zl + k))

    def router_third():
        landed(gz, gr.at[1])
        gtot[...] = gsum[...] + gz[0] + gz[1] + gz[2]
        for k in (1, 2, 3):
            go_on(gtot, gout.at[:, lane(x)], gs.at[2], gr.at[2], "dp",
                  place(x + k, zl))
        gout[:, lane(x)] = gtot[...]

    def router_last():
        landed(gz, gr.at[2])

    acts_first(0)
    part.reshape(2, rows, d)[0] = dot(hs[...], wts[2], ((1,), (1,))).astype(BF16)
    start_core(0)
    all_y(1, 2)
    y_first(0)
    y_pass(0, 2)
    y_start(0, 3)
    acts_second(0)
    y_pass(0, 1)
    y_start(0, 0)
    arrive_twin(1)
    hidden_back()
    acts_first(1)
    acts_first(2)
    pulls.first()
    y_pass(0, 3)
    y_end(0, 2)
    part.reshape(2, rows, d)[1] = (dot(dg[...], wts[0], ((1,), (1,)))
                                   + dot(du[...], wts[1], ((1,), (1,)))).astype(BF16)
    start_core(1)
    y_pass(0, 0)
    y_end(0, 1)
    y_first(1)
    pulls.second(3, 1)
    slice_twin(1)
    y_end(0, 3)
    slice_in(1)
    weight_rows(0)
    across_first(0)
    y_pass(1, 2)
    y_start(1, 3)
    y_end(0, 0)
    slice_twin(0)
    acts_second(1)
    y_pass(1, 1)
    y_start(1, 0)
    z_second(0)
    y_end(1, 2)
    pulls.second(2)
    y_pass(1, 3)
    acts_second(2)
    y_pass(1, 0)
    y_end(1, 1)
    pulls.third()
    slice_in(0)
    weight_rows(1)
    across_first(1)
    y_end(1, 3)
    pulls.last()
    router_first()
    across_second(0)
    weight_rows(2)
    router_second()
    across_first(2)
    y_end(1, 0)
    z_second(1)
    across_second(1)
    router_third()
    to[0] = z_third(0)
    total = z_third(1)
    ours = lax.broadcasted_iota(jnp.int32, (8, rows), 0) + 8 * j
    pick = lax.broadcasted_iota(jnp.int32, (8, rows), 1) == ours
    for e in range(8):
        weight = jnp.sum(jnp.where(pick, lt[e : e + 1, :], 0.0), axis=1, keepdims=True)
        total = total + weight * rt[e : e + 1, :]
    to[1] = total
    write(to, to_hbm, 3)
    router_last()
    write(gout, go_hbm, 4)
    for p in range(3):
        across_last(p)
    for a in range(2):
        gone(outs[a].reshape(GROUP, 8, d).at[pl.ds(0, GROUP - 1)], as_.at[a])
    marks.done()
    pulls.done()
    gone(slices.at[:, :, :, :, 0], es)
    gone(slices.at[:, :, :, :, 0], ts)
    gone(cbuf, cs)
    gone(cbuf.at[:, pl.ds(0, 3)], ys)
    gone(cbuf.at[:, 0, pl.ds(0, 3)], zs)
    gone(acts.at[pl.ds(0, 3)], xs)
    gone(zo.at[:, pl.ds(0, 3)], us)
    for i in range(3):
        gone(gz, gs.at[i])
    for copy in writes:
        copy.wait()


def layer(tokens, cotangent, routes, router_t, w_gate, w_up, w_down):
    d = tokens.shape[1]
    f = w_gate.shape[1]
    rows = GROUP * 8
    n = d // (NX * NL)
    cols = d // NX
    dma = pltpu.SemaphoreType.DMA
    return pl.pallas_call(
        layer_kernel,
        out_shape=[
            jax.ShapeDtypeStruct((3, n, f), F32),
            jax.ShapeDtypeStruct((2, 8, d), F32),
            jax.ShapeDtypeStruct((8, d), F32),
        ],
        in_specs=[ANY] * 7,
        out_specs=[ANY] * 3,
        scratch_shapes=[
            pltpu.VMEM((8, d), BF16),
            pltpu.VMEM((8, d), BF16),
            pltpu.VMEM(routes.shape, jnp.int32),
            pltpu.VMEM(router_t.shape, F32),
            pltpu.VMEM((3, NL, n, f), BF16),
            pltpu.VMEM((NL - 1, 8, cols), F32),
            pltpu.VMEM((3, n, f), F32),
            pltpu.VMEM((2, 8, d), F32),
            pltpu.VMEM((8, d), F32),
            pltpu.VMEM((NY, NZ, 2, 8, d), BF16),
            pltpu.VMEM((NY, NZ, 2, 8, d), BF16),
            pltpu.VMEM((GROUP, 8, 128), F32),
            pltpu.VMEM((8, 128), F32),
            pltpu.VMEM((GROUP, 1, rows), F32),
            pltpu.VMEM((1, rows), F32),
            pltpu.VMEM((3, d, f), BF16),
            pltpu.VMEM((rows, f), F32),
            pltpu.VMEM((rows, f), F32),
            pltpu.VMEM((rows, f), F32),
            pltpu.VMEM((NX, 3, rows, f), BF16),
            pltpu.VMEM((8, rows), F32),
            pltpu.VMEM((2, NY, NZ, 2, 8, d), BF16),
            pltpu.VMEM((2, NY, NZ, 8, d), BF16),
            pltpu.VMEM((2, NY, NZ, 8, d), BF16),
            pltpu.VMEM((2, NZ, 8, d), BF16),
            pltpu.VMEM((2, 2, NZ, 8, d), BF16),
            pltpu.VMEM((2, NZ, 8, d), BF16),
            pltpu.VMEM((2, 8, d), BF16),
            pltpu.VMEM((2, 2, 8, d), BF16),
            pltpu.VMEM((2, 8, d), BF16),
            pltpu.VMEM((3, NL, n, f), BF16),
            pltpu.VMEM((2, NX - 1, NY, NZ, 2, 8, cols), BF16),
            pltpu.VMEM((3, n, f), BF16),
            pltpu.VMEM((NX + 3, 8, cols), F32),
            pltpu.VMEM((8, cols), F32),
            pltpu.VMEM((8, cols), F32),
            dma((4,)), dma((5,)), dma((3,)), dma((2,)), dma((2, 8)), dma((2,)),
            dma, dma((8,)), dma, dma((8,)), dma((2,)),
            dma, dma((2, NY)), dma, dma((2, 2, NZ)), dma, dma((2, 2)),
            dma, dma((2,)), dma, dma((2,)),
            dma, dma((3, 2)), dma((3,)), dma, dma((3, 3)), dma((3,)), dma((3,)), dma((3,)),
        ],
        compiler_params=pltpu.CompilerParams(collective_id=0, has_side_effects=True),
        name="moe_layer",
    )(tokens, cotangent, routes, router_t, w_gate, w_up, w_down)


def finish_kernel(w, t, g, mo, to, go, o0, o1, o2):
    mo[...] = t[0].astype(BF16)
    to[...] = t[1].astype(BF16)
    go[...] = g[...]
    o0[...] = w[1]
    o1[...] = w[2]
    o2[...] = w[0]


def finish(w, t, g):
    grad = jax.ShapeDtypeStruct(w.shape[1:], F32)
    token = jax.ShapeDtypeStruct(t.shape[1:], BF16)
    return pl.pallas_call(
        finish_kernel,
        out_shape=[token, token, jax.ShapeDtypeStruct(g.shape, F32), grad, grad, grad],
        in_specs=[VMEM] * 3,
        out_specs=[VMEM] * 6,
        name="finish",
    )(w, t, g)


def local(tokens, routes, router, w_gate, w_up, w_down, cotangent):
    parts = layer(tokens, cotangent, routes, router.T, w_gate, w_up, w_down)
    mixed, grad_tokens, grad_router, grad_gate, grad_up, grad_down = finish(*parts)
    return (mixed, grad_tokens, grad_router.T, grad_gate, grad_up, grad_down)


def solution(mesh):
    return jax.shard_map(
        local,
        mesh=mesh,
        in_specs=(
            P(("dp", "expert"), None),
            P(("dp", "expert"), None),
            P(),
            P(None, "expert"),
            P(None, "expert"),
            P(None, "expert"),
            P(("dp", "expert"), None),
        ),
        out_specs=(
            P(("dp", "expert"), None),
            P(("dp", "expert"), None),
            P(),
            P("dp", "expert"),
            P("dp", "expert"),
            P("dp", "expert"),
        ),
        check_vma=False,
    )
```
